32 devices in a mesh: grp: 4 (over z), dev: 8 (over y, x, core).
Axes of the slice: x: 2, y: 2, z: 4, core: 2. Of those that a mesh axis runs over, the one named last changes fastest.
Arguments:
- positions: float32 [3, 128, 544], P(None, ('grp', 'dev')), may hold values from -2 to 20, as said below
- rest_shape: float32 [3, 544], replicated, may hold values from -3 to 3
- stiffness: float32 [544, 544], replicated, may hold values from -0.25 to 0.25
- up_map: float32 [544, 152], replicated, may hold values from -0.25 to 0.25
- down_map: float32 [152, 544], replicated, may hold values from -0.5 to 0.5
- m2m: float32 [152, 152], replicated, may hold values from -0.5 to 0.5
- box_template: float32 [3, 152], replicated, may hold values from -1 to 1
- near_target: int32 [32, 2], P(('grp', 'dev')), may hold values from 0 to 3
- near_owner: int32 [32, 2], P(('grp', 'dev')), may hold values from 0 to 7, as said below
- near_cell: int32 [32, 2], P(('grp', 'dev')), may hold values from 0 to 3, as said below
- near_count: int32 [32], P(('grp', 'dev')), may hold values from 1 to 2, as said below
Outputs:
- new_positions: float32 [3, 128, 544], P(None, ('grp', 'dev'))
- velocity: float32 [3, 128, 544], P(None, ('grp', 'dev'))
The draws below stay inside these ranges and needn't reach their ends.
Inputs may be any that keep to these rules, and one draw needn't show every extreme that they name: `positions`: each cell's points lie within about 1.2 of the cell's center; devices of one group sit on a grid of spacing 2.5, groups are 6 apart. `near_owner`: device e's slots name devices of e's own group other than e itself; at most 2 used slots of one device name the same owner, and device 0 uses all 2 slots with exactly 2 on each owner it names. `near_cell`: the source cells named by one device's used slots are distinct. `near_count`: the used slots come first; device 0 uses all of them.
All inputs are finite; a program needn't handle non-finite values.
Results may differ from the reference program's by a relative error of at most 0.0003.
Values sent between devices are 32-bit elements; how exact they have to be, the bound alone decides.
No kernel may reach another device: no remote copies, remote signals or barrier semaphores. Data moves between devices by JAX's collectives and lax.ppermute only.
A program may use at most 64 MiB of HBM per device.

```python
import jax
import jax.numpy as jnp
from jax import lax

P_SIZE = 544
Q = 152
CELLS_DEV = 4
NEAR = 2
CAP = 2
STEPS = 2
N_GRP = 4
N_DEV = 8


def near_lists(key):
    devices = N_GRP * N_DEV
    pair_count = NEAR // CAP
    key_owner, key_cell, key_order, key_count = jax.random.split(key, 4)
    device_ids = jnp.arange(devices, dtype=jnp.int32)
    scores = jax.random.randint(key_owner, (devices, N_DEV - 1), 0, 2 ** 20) * N_DEV + jnp.arange(N_DEV - 1, dtype=jnp.int32)[None, :]
    offsets = jnp.argsort(scores, axis=1)[:, :pair_count].astype(jnp.int32)
    owners = (device_ids[:, None] % N_DEV + 1 + offsets) % N_DEV
    owners = jnp.repeat(owners, CAP, axis=1)
    cell_scores = jax.random.randint(key_cell, (devices, pair_count, CELLS_DEV), 0, 2 ** 20) * CELLS_DEV + jnp.arange(CELLS_DEV, dtype=jnp.int32)[None, None, :]
    cell_ids = jnp.argsort(cell_scores, axis=2)[:, :, :CAP].reshape(devices, NEAR).astype(jnp.int32)
    order_scores = jax.random.randint(key_order, (devices, NEAR), 0, 2 ** 20) * NEAR + jnp.arange(NEAR, dtype=jnp.int32)[None, :]
    slot_order = jnp.argsort(order_scores, axis=1)
    owners = jnp.take_along_axis(owners, slot_order, axis=1).astype(jnp.int32)
    cell_ids = jnp.take_along_axis(cell_ids, slot_order, axis=1).astype(jnp.int32)
    counts = jax.random.randint(key_count, (devices,), 1, NEAR + 1).astype(jnp.int32)
    counts = counts.at[0].set(NEAR)
    return (owners, cell_ids, counts)


def draw_near_owner(key, part):
    return near_lists(jax.random.fold_in(key, 7))[0]


def draw_near_cell(key, part):
    return near_lists(jax.random.fold_in(key, 7))[1]


def draw_near_count(key, part):
    return near_lists(jax.random.fold_in(key, 7))[2]


def draw_positions(key, part):
    devices = N_GRP * N_DEV
    total = CELLS_DEV * devices
    cell_index = jnp.arange(total, dtype=jnp.int32)
    device_ids = cell_index // CELLS_DEV
    group_index = device_ids // N_DEV
    within = device_ids % N_DEV
    key_center, key_shape, key_rough = jax.random.split(jax.random.fold_in(key, 3), 3)
    grid = jnp.stack([2.5 * (within % 8).astype(jnp.float32), 2.5 * (within // 8).astype(jnp.float32), 6.0 * group_index.astype(jnp.float32)])
    centers = grid + jax.random.uniform(key_center, (3, total), jnp.float32, -0.5, 0.5)
    direction = jax.random.normal(key_shape, (3, total, P_SIZE), jnp.float32)
    direction = direction / jnp.sqrt(jnp.sum(direction * direction, axis=0, keepdims=True) + 0.1)
    roughness = 0.08 * jax.random.normal(key_rough, (3, total, P_SIZE), jnp.float32)
    return centers[:, :, None] + direction * (1.0 + roughness)


def with_ends(entries, rng, low, high):
    shape = entries.shape
    spot = [jax.random.randint(jax.random.fold_in(rng, axis), (), 0, shape[axis]) for axis in range(len(shape))]
    entries = entries.at[tuple(spot)].set(low)
    longest = shape.index(max(shape))
    spot[longest] = (spot[longest] + 1) % shape[longest]
    return entries.at[tuple(spot)].set(high)


def gaussian(own_key, dims, spread, most, held_as=jnp.bfloat16):
    values = spread * jax.random.normal(own_key, dims, jnp.float32)
    return jnp.clip(values, min=-most, max=most).astype(held_as)


def setup_inputs(seed: int = 0) -> dict:
    seeds = jax.random.split(jax.random.key(seed), 12)
    positions = draw_positions(jax.random.fold_in(seeds[11], 71), 0)
    rest_shape = gaussian(seeds[1], (3, P_SIZE), 0.5, 3.0, jnp.float32)
    stiffness = gaussian(seeds[2], (P_SIZE, P_SIZE), P_SIZE ** -0.5, 0.25, jnp.float32)
    up_map = gaussian(seeds[3], (P_SIZE, Q), P_SIZE ** -0.5, 0.25, jnp.float32)
    down_map = gaussian(seeds[4], (Q, P_SIZE), Q ** -0.5, 0.5, jnp.float32)
    m2m = gaussian(seeds[5], (Q, Q), Q ** -0.5, 0.5, jnp.float32)
    box_template = jnp.clip(jax.random.uniform(seeds[6], (3, Q), jnp.float32, -1.0, 1.0), -1.0, 1.0)
    near_target = with_ends(jax.random.randint(seeds[7], (N_GRP * N_DEV, NEAR), 0, CELLS_DEV), jax.random.fold_in(seeds[7], 1), 0, CELLS_DEV - 1).astype(jnp.int32)
    near_owner = draw_near_owner(jax.random.fold_in(seeds[11], 71), 0)
    near_cell = draw_near_cell(jax.random.fold_in(seeds[11], 71), 0)
    near_count = draw_near_count(jax.random.fold_in(seeds[11], 71), 0)
    return {"positions": positions, "rest_shape": rest_shape, "stiffness": stiffness, "up_map": up_map, "down_map": down_map, "m2m": m2m, "box_template": box_template, "near_target": near_target, "near_owner": near_owner, "near_cell": near_cell, "near_count": near_count}


EPSILON_SQ = 0.25
VISCOSITY = 0.039788735772973836
TIME_STEP = 0.1
SKALAK_HARDEN = 2.0
CHECK_RADIUS = 1.0
DEVICE_RADIUS = 1.5
GROUP_RADIUS = 6.0

def stokes(targets, sources, forces):
    delta_x = targets[0][:, None] - sources[0][None, :]
    delta_y = targets[1][:, None] - sources[1][None, :]
    delta_z = targets[2][:, None] - sources[2][None, :]
    square = delta_x * delta_x + delta_y * delta_y + delta_z * delta_z
    inverse = 1.0 / ((square + EPSILON_SQ) * jnp.sqrt(square + EPSILON_SQ))
    direct = (square + 2.0 * EPSILON_SQ) * inverse
    projected = (delta_x * forces[0][None, :] + delta_y * forces[1][None, :] + delta_z * forces[2][None, :]) * inverse
    result = jnp.einsum('ts,ks->kt', direct, forces, precision=lax.Precision.HIGHEST)
    extra = jnp.stack([lax.optimization_barrier(jnp.sum(delta_x * projected, axis=1)), lax.optimization_barrier(jnp.sum(delta_y * projected, axis=1)), lax.optimization_barrier(jnp.sum(delta_z * projected, axis=1))])
    return VISCOSITY * (result + extra)

def membrane(points, rest_shape, stiffness):
    centroid = lax.optimization_barrier(jnp.mean(points, axis=2, keepdims=True))
    strain = points - centroid - rest_shape[:, None, :]
    linear = jnp.dot(strain.reshape(-1, strain.shape[2]), stiffness, precision=lax.Precision.HIGHEST).reshape(strain.shape)
    stretch = lax.optimization_barrier(jnp.sum(linear * linear, axis=0))
    return -linear * (1.0 + SKALAK_HARDEN * stretch / (1.0 + stretch))

def box_far(checks, equivalents, centers, radius, weights, box_template):
    sources = centers[:, :, None] + radius * box_template[None]
    forces = equivalents * weights.astype(equivalents.dtype)[:, None, None]
    source_count = equivalents.shape[0] * equivalents.shape[2]
    flat_sources = jnp.transpose(sources, (1, 0, 2)).reshape(3, source_count)
    flat_forces = jnp.transpose(forces, (1, 0, 2)).reshape(3, source_count)
    return stokes(checks, flat_sources, flat_forces)

def reference(positions, rest_shape, stiffness, up_map, down_map, m2m, box_template, near_target, near_owner, near_cell, near_count):
    devices = N_GRP * N_DEV
    device_ids = jnp.arange(devices, dtype=jnp.int32)
    group_of = device_ids // N_DEV
    source_cells = ((group_of[:, None] * N_DEV + near_owner) * CELLS_DEV + near_cell).astype(jnp.int32)
    target_cells = (device_ids[:, None] * CELLS_DEV + near_target).astype(jnp.int32)
    in_use = jnp.arange(NEAR, dtype=jnp.int32)[None, :] < near_count[:, None]
    onehot = ((near_target[:, :, None] == jnp.arange(CELLS_DEV, dtype=jnp.int32)[None, None, :]) & in_use[:, :, None]).astype(positions.dtype)
    points = positions
    velocity = jnp.zeros_like(positions)
    for step_index in range(STEPS):
        forces = membrane(points, rest_shape, stiffness)
        by_points = points.reshape(3, devices, CELLS_DEV, P_SIZE)
        by_forces = forces.reshape(3, devices, CELLS_DEV, P_SIZE)
        summed = jnp.transpose(lax.optimization_barrier(jnp.sum(by_forces, axis=2)), (1, 0, 2)).reshape(devices * 3, P_SIZE)
        equivalents = jnp.dot(summed, up_map, precision=lax.Precision.HIGHEST).reshape(devices, 3, Q)
        centers = jnp.transpose(lax.optimization_barrier(jnp.mean(by_points, axis=(2, 3))))
        grouped = equivalents.reshape(N_GRP, N_DEV, 3, Q)
        placed = centers.reshape(N_GRP, N_DEV, 3)
        group_sums = lax.optimization_barrier(jnp.sum(grouped, axis=1)).reshape(N_GRP * 3, Q)
        group_eq = jnp.dot(group_sums, m2m, precision=lax.Precision.HIGHEST).reshape(N_GRP, 3, Q)
        group_centers = lax.optimization_barrier(jnp.mean(placed, axis=1))

        def far_one(device):
            group_index = device // N_DEV
            within = device % N_DEV
            checks = centers[device][:, None] + CHECK_RADIUS * box_template
            inner_far = box_far(checks, grouped[group_index], placed[group_index], DEVICE_RADIUS, jnp.arange(N_DEV, dtype=jnp.int32) != within, box_template)
            outer_far = box_far(checks, group_eq, group_centers, GROUP_RADIUS, jnp.arange(N_GRP, dtype=jnp.int32) != group_index, box_template)
            return inner_far + outer_far
        far_checks = lax.map(far_one, device_ids)
        far_surface = jnp.dot(far_checks.reshape(devices * 3, Q), down_map, precision=lax.Precision.HIGHEST).reshape(devices, 3, P_SIZE)
        stacked = jnp.concatenate([points, forces], axis=0)

        def near_one(device):
            sources = stacked[:, source_cells[device]]
            receivers = points[:, target_cells[device]]
            near_tiles = jax.vmap(stokes, in_axes=(1, 1, 1), out_axes=1)(receivers, sources[:3], sources[3:])
            return jnp.einsum('ksp,sc->kcp', near_tiles, onehot[device], precision=lax.Precision.HIGHEST)
        near_velocity = jnp.transpose(lax.map(near_one, device_ids), (1, 0, 2, 3))
        velocity = (jnp.transpose(far_surface, (1, 0, 2))[:, :, None, :] + near_velocity).reshape(3, CELLS_DEV * devices, P_SIZE)
        points = points + TIME_STEP * velocity
    return (points, velocity)
```

```python
import jax
import jax.numpy as jnp
from jax import lax
from jax.sharding import PartitionSpec as P

NEAR = 2
STEPS = 2


EPSILON_SQ = 0.25
VISCOSITY = 0.039788735772973836
TIME_STEP = 0.1
SKALAK_HARDEN = 2.0
CHECK_RADIUS = 1.0
DEVICE_RADIUS = 1.5
GROUP_RADIUS = 6.0


def stokes(targets, sources, forces):
    delta_x = targets[0][:, None] - sources[0][None, :]
    delta_y = targets[1][:, None] - sources[1][None, :]
    delta_z = targets[2][:, None] - sources[2][None, :]
    square = delta_x * delta_x + delta_y * delta_y + delta_z * delta_z
    inverse = 1.0 / ((square + EPSILON_SQ) * jnp.sqrt(square + EPSILON_SQ))
    direct = (square + 2.0 * EPSILON_SQ) * inverse
    projected = (
        delta_x * forces[0][None, :] + delta_y * forces[1][None, :] + delta_z * forces[2][None, :]
    ) * inverse
    result = jnp.einsum("ts,ks->kt", direct, forces, precision=lax.Precision.HIGHEST)
    extra = jnp.stack(
        [
            jnp.sum(delta_x * projected, axis=1),
            jnp.sum(delta_y * projected, axis=1),
            jnp.sum(delta_z * projected, axis=1),
        ]
    )
    return VISCOSITY * (result + extra)


def membrane(points, rest_shape, stiffness):
    centroid = jnp.mean(points, axis=2, keepdims=True)
    strain = points - centroid - rest_shape[:, None, :]
    linear = jnp.dot(
        strain.reshape(-1, strain.shape[2]), stiffness, precision=lax.Precision.HIGHEST
    ).reshape(strain.shape)
    stretch = jnp.sum(linear * linear, axis=0)
    return -linear * (1.0 + SKALAK_HARDEN * stretch / (1.0 + stretch))


def box_far(checks, equivalents, centers, radius, weights, box_template):
    sources = centers[:, :, None] + radius * box_template[None]
    forces = equivalents * weights.astype(equivalents.dtype)[:, None, None]
    source_count = equivalents.shape[0] * equivalents.shape[2]
    flat_sources = jnp.transpose(sources, (1, 0, 2)).reshape(3, source_count)
    flat_forces = jnp.transpose(forces, (1, 0, 2)).reshape(3, source_count)
    return stokes(checks, flat_sources, flat_forces)


def body(
    positions,
    rest_shape,
    stiffness,
    up_map,
    down_map,
    m2m,
    box_template,
    near_target,
    near_owner,
    near_cell,
    near_count,
):
    own_device = lax.axis_index("dev")
    own_group = lax.axis_index("grp")
    dev_count = lax.axis_size("dev")
    cell_count = positions.shape[1]
    slot_ids = jnp.arange(NEAR, dtype=jnp.int32)
    owners = near_owner[0]
    cell_ids = near_cell[0]
    targets = near_target[0]
    in_use = slot_ids < near_count[0]
    onehot = (
        (targets[:, None] == jnp.arange(cell_count, dtype=jnp.int32)[None, :]) & in_use[:, None]
    ).astype(jnp.float32)
    points = positions
    velocity = jnp.zeros_like(positions)
    groups = lax.axis_size("grp")
    q = up_map.shape[1]
    for step_index in range(STEPS):
        pool = lax.all_to_all(
            jnp.broadcast_to(points[None], (dev_count,) + points.shape), "dev", 0, 0
        )
        sources = pool[owners, :, cell_ids]
        source_points = jnp.transpose(sources, (1, 0, 2))
        source_forces = membrane(source_points, rest_shape, stiffness)
        receivers = jnp.take(points, targets, axis=1)
        near_tiles = jax.vmap(stokes, in_axes=(1, 1, 1), out_axes=1)(
            receivers, source_points, source_forces
        )
        near_velocity = jnp.einsum(
            "ksp,sc->kcp", near_tiles, onehot, precision=lax.Precision.HIGHEST
        )
        forces = membrane(points, rest_shape, stiffness)
        equivalent = jnp.dot(jnp.sum(forces, axis=1), up_map, precision=lax.Precision.HIGHEST)
        center = jnp.mean(points, axis=(1, 2))
        checks = center[:, None] + CHECK_RADIUS * box_template
        message = jnp.concatenate([equivalent.reshape(-1), center])
        size = -(-message.shape[0] // 512) * 512
        message = jnp.pad(message, (0, size - message.shape[0]))
        told = lax.all_to_all(
            jnp.broadcast_to(message[None], (groups * dev_count, size)), ("grp", "dev"), 0, 0
        )
        all_forces = told[:, : 3 * q].reshape(groups, dev_count, 3, q)
        all_places = told[:, 3 * q : 3 * q + 3].reshape(groups, dev_count, 3)
        box_forces = all_forces[own_group]
        places = all_places[own_group]
        indices = jnp.arange(dev_count, dtype=jnp.int32)
        added = box_far(
            checks, box_forces, places, DEVICE_RADIUS, indices != own_device, box_template
        )
        group_eq = jnp.dot(
            jnp.sum(all_forces, axis=1).reshape(groups * 3, q), m2m, precision=lax.Precision.HIGHEST
        ).reshape(groups, 3, q)
        outer_indices = jnp.arange(groups, dtype=jnp.int32)
        outer_far = box_far(
            checks,
            group_eq,
            jnp.mean(all_places, axis=1),
            GROUP_RADIUS,
            outer_indices != own_group,
            box_template,
        )
        far_checks = added + outer_far
        far_surface = jnp.dot(far_checks, down_map, precision=lax.Precision.HIGHEST)
        velocity = far_surface[:, None, :] + near_velocity
        points = points + TIME_STEP * velocity
    return (points, velocity)


def solution(mesh):
    return jax.shard_map(
        body,
        mesh=mesh,
        in_specs=(
            P(None, ("grp", "dev"), None),
            P(),
            P(),
            P(),
            P(),
            P(),
            P(),
            P(("grp", "dev"), None),
            P(("grp", "dev"), None),
            P(("grp", "dev"), None),
            P(("grp", "dev")),
        ),
        out_specs=(P(None, ("grp", "dev"), None), P(None, ("grp", "dev"), None)),
        check_vma=False,
    )
```

```python
import functools

import jax
import jax.numpy as jnp
from jax import lax
from jax.experimental import pallas as pl
from jax.experimental.pallas import tpu as pltpu
from jax.sharding import PartitionSpec as P

STEPS = 2
NEAR = 2

EPSILON_SQ = 0.25
VISCOSITY = 0.039788735772973836
TIME_STEP = 0.1
SKALAK_HARDEN = 2.0
CHECK_RADIUS = 1.0
DEVICE_RADIUS = 1.5
GROUP_RADIUS = 6.0

LANES = 128
SUB = 8


def up8(n):
    return -(-n // SUB) * SUB


def split(a):
    high = a.astype(jnp.bfloat16)
    low = (a - high.astype(jnp.float32)).astype(jnp.bfloat16)
    return high, low


def dot3(a, b):
    a_high, a_low = split(a)
    b_high, b_low = split(b)
    dot = functools.partial(jnp.dot, preferred_element_type=jnp.float32)
    return dot(a_high, b_high) + (dot(a_low, b_high) + dot(a_high, b_low))


def harden(linear, stretch):
    return -linear * (1.0 + SKALAK_HARDEN * stretch / (1.0 + stretch))


def add_pair(acc, delta, force):
    square = delta[0] * delta[0] + delta[1] * delta[1] + delta[2] * delta[2]
    root = lax.rsqrt(square + EPSILON_SQ)
    inverse = root * root * root
    direct = root + EPSILON_SQ * inverse
    along = (delta[0] * force[0] + delta[1] * force[1] + delta[2] * force[2]) * inverse
    return [acc[k] + (direct * force[k] + along * delta[k]) for k in range(3)]


def membrane_kernel(points_ref, rest_ref, stiffness_ref, up_ref, out_ref, rows_ref, flat_ref):
    cells, size = points_ref.shape[1:]
    q = up_ref.shape[1]
    tail = q - LANES
    rows_ref[...] = jnp.zeros_like(rows_ref)
    centers = []
    for k in range(3):
        own = points_ref[k]
        mean = jnp.mean(own, axis=1, keepdims=True)
        rows_ref[SUB * k : SUB * k + cells, :] = own - mean - rest_ref[k : k + 1, :]
        centers.append(jnp.mean(mean, axis=0, keepdims=True))
    linear = dot3(rows_ref[...], stiffness_ref[...])
    parts = [linear[SUB * k : SUB * (k + 1)] for k in range(3)]
    stretch = parts[0] * parts[0] + parts[1] * parts[1] + parts[2] * parts[2]
    sums = [jnp.sum(harden(part, stretch), axis=0, keepdims=True) for part in parts]
    summed = jnp.concatenate(sums + [jnp.zeros((SUB - 3, size), jnp.float32)], axis=0)
    flat_ref[...] = jnp.zeros_like(flat_ref)
    flat_ref[:, :q] = dot3(summed, up_ref[...])
    ends = flat_ref[:, LANES:]
    last = ends[0:1]
    lane = lax.broadcasted_iota(jnp.int32, (1, LANES), 1)
    for k in range(1, 3):
        last = last + pltpu.roll(ends[k : k + 1], tail * k, axis=1)
    for k in range(3):
        last = jnp.where(lane == 3 * tail + k, centers[k], last)
    message = jnp.concatenate([flat_ref[0:3, :LANES], last], axis=0)
    out_ref[...] = jnp.broadcast_to(message[None], out_ref.shape)


def pick(block, row):
    rows = lax.broadcasted_iota(jnp.int32, (block.shape[0], 1), 0)
    return jnp.sum(jnp.where(rows == row, block, 0.0), axis=0, keepdims=True)


def near_kernel(
    target_ref,
    owner_ref,
    cell_ref,
    count_ref,
    own_ref,
    *refs,
    spread,
):
    pool_refs, (rest_ref, stiffness_ref, out_ref, rows_ref, cols_ref, aim_ref, move_ref) = (
        refs[:-7],
        refs[-7:],
    )
    size = own_ref.shape[2]
    chunks = aim_ref.shape[1] // LANES
    me = lax.axis_index("dev")
    out_ref[...] = jnp.zeros_like(out_ref)
    rows_ref[...] = jnp.zeros_like(rows_ref)
    move_ref[...] = jnp.zeros_like(move_ref)
    for slot in range(NEAR):
        cell = cell_ref[0, slot]
        owner = owner_ref[0, slot]
        if spread:
            for mask, pool_ref in enumerate(pool_refs):

                @pl.when((owner ^ me) == mask)
                def _(pool_ref=pool_ref):
                    for k in range(3):
                        rows_ref[SUB * slot + k : SUB * slot + k + 1, :] = pick(pool_ref[k], cell)
        else:
            for k in range(3):
                rows_ref[SUB * slot + k : SUB * slot + k + 1, :] = pick(
                    pool_refs[0][owner, k], cell
                )
    sources = rows_ref[...]
    for slot in range(NEAR):
        own = sources[SUB * slot : SUB * slot + 3]
        mean = jnp.mean(own, axis=1, keepdims=True)
        move_ref[SUB * slot : SUB * slot + 3, :] = own - mean - rest_ref[...]
    linear = dot3(move_ref[...], stiffness_ref[...])
    square = linear * linear
    for slot in range(NEAR):
        part = linear[SUB * slot : SUB * slot + 3]
        stretch = jnp.sum(square[SUB * slot : SUB * slot + 3], axis=0, keepdims=True)
        rows_ref[SUB * slot + 3 : SUB * slot + 6, :] = harden(part, stretch)
    aim_ref[...] = jnp.zeros_like(aim_ref)
    for slot in range(NEAR):

        @pl.when(slot < count_ref[0])
        def _(slot=slot):
            target = target_ref[0, slot]
            cols_ref[...] = jnp.transpose(rows_ref[SUB * slot : SUB * slot + SUB, :])
            for k in range(3):
                aim_ref[k : k + 1, :size] = pick(own_ref[k], target)
            aims = [
                [
                    jnp.broadcast_to(aim_ref[k : k + 1, LANES * c : LANES * (c + 1)], (SUB, LANES))
                    for k in range(3)
                ]
                for c in range(chunks)
            ]

            def group(i, acc):
                block = cols_ref[pl.ds(pl.multiple_of(i * SUB, SUB), SUB), :]
                place = [jnp.broadcast_to(block[:, k : k + 1], (SUB, LANES)) for k in range(3)]
                force = [jnp.broadcast_to(block[:, k : k + 1], (SUB, LANES)) for k in range(3, 6)]
                return tuple(
                    tuple(
                        add_pair(acc[c], [aims[c][k] - place[k] for k in range(3)], force)
                    )
                    for c in range(chunks)
                )

            zero = jnp.zeros((SUB, LANES), jnp.float32)
            acc = lax.fori_loop(
                0, size // SUB, group, tuple((zero,) * 3 for _ in range(chunks)), unroll=2
            )
            for c in range(chunks):
                for k in range(3):
                    part = VISCOSITY * jnp.sum(acc[c][k], axis=0, keepdims=True)
                    aim_ref[k : k + 1, LANES * c : LANES * (c + 1)] = part
            for k in range(3):
                old = out_ref[k]
                chosen = lax.broadcasted_iota(jnp.int32, (old.shape[0], 1), 0) == target
                out_ref[k] = old + jnp.where(chosen, aim_ref[k : k + 1, :size], 0.0)


def boxes(main, ends, center, template, radius, per_row):
    count = main[0].shape[0]
    tail_lanes = template[2]
    rows = []
    for k in range(3):
        place_main = center[k] + radius * template[0][k : k + 1]
        place_ends = jnp.where(tail_lanes, center[k] + radius * template[1][k : k + 1], 0.0)
        rows.append((place_main, place_ends))
    for k in range(3):
        rows.append((main[k], ends[k]))
    packed = []
    for whole, part in rows:
        turn = lax.broadcasted_iota(jnp.int32, (count, 1), 0) % per_row[0]
        shifted = jnp.where(turn == 0, part, 0.0)
        for i in range(1, per_row[0]):
            shifted += jnp.where(turn == i, pltpu.roll(part, per_row[1] * i, axis=1), 0.0)
        packed.append(
            [whole]
            + [
                jnp.sum(shifted[a : min(a + per_row[0], count)], axis=0, keepdims=True)
                for a in range(0, count, per_row[0])
            ]
        )
    return packed


def far_kernel(
    told_ref,
    points_ref,
    near_ref,
    m2m_ref,
    template_ref,
    down_ref,
    points_out_ref,
    velocity_ref,
    wide_ref,
    sums_ref,
    group_ref,
    source_ref,
    check_ref,
    result_ref,
    *,
    groups,
    devs,
):
    q = template_ref.shape[1]
    tail = q - LANES
    per_row = (LANES // tail, tail)
    group = lax.axis_index("grp")
    dev = lax.axis_index("dev")
    lane = lax.broadcasted_iota(jnp.int32, (1, LANES), 1)
    tail_lanes = lane < tail

    def ends_of(row, k):
        moved = pltpu.roll(row, LANES - tail * k, axis=1) if k else row
        return jnp.where(tail_lanes, moved, 0.0)

    wide_ref[...] = jnp.zeros_like(wide_ref)
    wide_ref[0:3, :q] = template_ref[...]
    template = (wide_ref[:, :LANES], wide_ref[:, LANES:], tail_lanes)

    first = group * devs
    own_rows = [told_ref[pl.ds(first, devs), k, :] for k in range(4)]
    others = lax.broadcasted_iota(jnp.int32, (devs, 1), 0) != dev
    inner = boxes(
        [jnp.where(others, own_rows[k], 0.0) for k in range(3)],
        [jnp.where(others, ends_of(own_rows[3], k), 0.0) for k in range(3)],
        [own_rows[3][:, 3 * tail + k : 3 * tail + k + 1] for k in range(3)],
        template,
        DEVICE_RADIUS,
        per_row,
    )

    span = up8(groups)
    sums_ref[...] = jnp.zeros_like(sums_ref)
    for h in range(groups):
        sums_ref[h] = jnp.sum(told_ref[h * devs : (h + 1) * devs], axis=0)
    sum_rows = [sums_ref[:, k, :] for k in range(4)]
    for k in range(3):
        group_ref[span * k : span * (k + 1), :LANES] = sum_rows[k]
        group_ref[span * k : span * (k + 1), LANES:] = ends_of(sum_rows[3], k)
    shifted = dot3(group_ref[:, :q], m2m_ref[...])
    group_ref[:, :q] = shifted
    other_groups = lax.broadcasted_iota(jnp.int32, (span, 1), 0) != group
    outer = boxes(
        [
            jnp.where(other_groups, group_ref[span * k : span * (k + 1), :LANES], 0.0)
            for k in range(3)
        ],
        [
            jnp.where(other_groups, group_ref[span * k : span * (k + 1), LANES:], 0.0)
            for k in range(3)
        ],
        [sum_rows[3][:, 3 * tail + k : 3 * tail + k + 1] / devs for k in range(3)],
        template,
        GROUP_RADIUS,
        per_row,
    )
    rows = 0
    for part, count in ((inner, devs), (outer, groups)):
        ends = -(-count // per_row[0])
        for index in range(6):
            source_ref[index, rows : rows + count, :] = part[index][0][:count]
            for j in range(ends):
                source_ref[index, rows + count + j : rows + count + j + 1, :] = part[index][1 + j]
        rows += count + ends

    center_row = told_ref[pl.ds(first + dev, 1), 3, :]
    for k in range(3):
        center = center_row[:, 3 * tail + k : 3 * tail + k + 1]
        wide_ref[k : k + 1, :] = center + CHECK_RADIUS * wide_ref[k : k + 1, :]
    check_ref[...] = jnp.transpose(wide_ref[...])

    @pl.loop(0, q // SUB)
    def _(i):
        at = pl.ds(pl.multiple_of(i * SUB, SUB), SUB)
        block = check_ref[at, :]
        check = [jnp.broadcast_to(block[:, k : k + 1], (SUB, LANES)) for k in range(3)]
        acc = [jnp.zeros((SUB, LANES), jnp.float32)] * 3
        for row in range(rows):
            source = [
                jnp.broadcast_to(source_ref[index, row : row + 1, :], (SUB, LANES))
                for index in range(6)
            ]
            acc = add_pair(acc, [check[k] - source[k] for k in range(3)], source[3:])
        total = [VISCOSITY * jnp.sum(acc[k], axis=1, keepdims=True) for k in range(3)]
        result_ref[at, :] = jnp.where(
            lane == 0, total[0], jnp.where(lane == 1, total[1], total[2])
        )

    checks = jnp.transpose(result_ref[...])[:SUB]
    surface = dot3(checks, down_ref[...])
    for k in range(3):
        velocity = surface[k : k + 1] + near_ref[k]
        velocity_ref[k] = velocity
        points_out_ref[k] = points_ref[k] + TIME_STEP * velocity


VMEM = pl.BlockSpec(memory_space=pltpu.VMEM)
SMEM = pl.BlockSpec(memory_space=pltpu.SMEM)


def float32(*shape):
    return jax.ShapeDtypeStruct(shape, jnp.float32)


def body(
    positions,
    rest_shape,
    stiffness,
    up_map,
    down_map,
    m2m,
    box_template,
    near_target,
    near_owner,
    near_cell,
    near_count,
):
    devs = lax.axis_size("dev")
    groups = lax.axis_size("grp")
    cells, size = positions.shape[1:]
    q = up_map.shape[1]
    wide = -(-size // LANES) * LANES
    spread = devs == 8
    span = up8(groups)
    tail_boxes = LANES // (q - LANES)
    source_rows = devs + groups + -(-devs // tail_boxes) + -(-groups // tail_boxes)

    membrane = pl.pallas_call(
        membrane_kernel,
        out_shape=float32(groups * devs, 4, LANES),
        in_specs=[VMEM] * 4,
        out_specs=VMEM,
        scratch_shapes=[
            pltpu.VMEM((3 * SUB, size), jnp.float32),
            pltpu.VMEM((SUB, 2 * LANES), jnp.float32),
        ],
        name="membrane",
        cost_estimate=pl.CostEstimate(flops=10**9, bytes_accessed=10**6, transcendentals=0),
    )
    pools = 8 if spread else 1
    near = pl.pallas_call(
        functools.partial(near_kernel, spread=spread),
        out_shape=float32(3, cells, size),
        in_specs=[SMEM] * 4 + [VMEM] * (1 + pools + 2),
        out_specs=VMEM,
        scratch_shapes=[
            pltpu.VMEM((NEAR * SUB, size), jnp.float32),
            pltpu.VMEM((size, SUB), jnp.float32),
            pltpu.VMEM((SUB, wide), jnp.float32),
            pltpu.VMEM((NEAR * SUB, size), jnp.float32),
        ],
        name="near",
        cost_estimate=pl.CostEstimate(flops=4 * 10**9, bytes_accessed=10**6, transcendentals=0),
    )
    far = pl.pallas_call(
        functools.partial(far_kernel, groups=groups, devs=devs),
        out_shape=(float32(3, cells, size), float32(3, cells, size)),
        in_specs=[VMEM] * 6,
        out_specs=(VMEM, VMEM),
        scratch_shapes=[
            pltpu.VMEM((SUB, 2 * LANES), jnp.float32),
            pltpu.VMEM((span, 4, LANES), jnp.float32),
            pltpu.VMEM((3 * span, 2 * LANES), jnp.float32),
            pltpu.VMEM((6, up8(source_rows), LANES), jnp.float32),
            pltpu.VMEM((2 * LANES, SUB), jnp.float32),
            pltpu.VMEM((q, LANES), jnp.float32),
        ],
        name="far",
        cost_estimate=pl.CostEstimate(flops=2 * 10**9, bytes_accessed=10**6, transcendentals=0),
    )

    def to(array, mask):
        return lax.ppermute(array, "dev", [(j, j ^ mask) for j in range(devs)])

    points = positions
    velocity = None
    for _ in range(STEPS):
        message = membrane(points, rest_shape, stiffness, up_map)
        told = lax.all_to_all(message, ("grp", "dev"), 0, 0)
        if spread:
            pool = [points] + [to(points, mask) for mask in (2, 4, 6)]
            pool += [to(array, 1) for array in pool]
            pool = [pool[mask // 2 + 4 * (mask % 2)] for mask in range(8)]
        else:
            copies = jnp.broadcast_to(points[None], (devs,) + points.shape)
            pool = [lax.all_to_all(copies, "dev", 0, 0)]
        close = near(
            near_target,
            near_owner,
            near_cell,
            near_count,
            points,
            *pool,
            rest_shape,
            stiffness,
        )
        points, velocity = far(told, points, close, m2m, box_template, down_map)
    return (points, velocity)


def solution(mesh):
    both = ("grp", "dev")
    return jax.shard_map(
        body,
        mesh=mesh,
        in_specs=(P(None, both, None),) + (P(),) * 6 + (P(both, None),) * 3 + (P(both),),
        out_specs=(P(None, both, None), P(None, both, None)),
        check_vma=False,
    )
```

```python
import functools

import jax
import jax.numpy as jnp
from jax import lax
from jax.experimental import pallas as pl
from jax.experimental.pallas import tpu as pltpu
from jax.sharding import PartitionSpec as P


STEPS = 2
NEAR = 2

EPSILON_SQ = 0.25
VISCOSITY = 0.039788735772973836
TIME_STEP = 0.1
SKALAK_HARDEN = 2.0
CHECK_RADIUS = 1.0
DEVICE_RADIUS = 1.5
GROUP_RADIUS = 6.0

LANES = 128
SUB = 8
CHUNK = 544
BATCH = 3


def up8(n):
    return -(-n // SUB) * SUB


def split(a):
    high = a.astype(jnp.bfloat16)
    low = (a - high.astype(jnp.float32)).astype(jnp.bfloat16)
    return high, low


NN = (((1,), (0,)), ((), ()))
NT = (((1,), (1,)), ((), ()))


def dot3(a, b_parts, dims=NN):
    dot = functools.partial(
        lax.dot_general, dimension_numbers=dims, preferred_element_type=jnp.float32
    )
    rows = a.shape[0]
    first = a.astype(jnp.bfloat16).astype(jnp.float32)
    both = jnp.concatenate([first, a - first], axis=0).astype(jnp.bfloat16)
    high = dot(both, b_parts[0])
    return high[:rows] + (high[rows:] + dot(first.astype(jnp.bfloat16), b_parts[1]))


def harden(linear, stretch):
    return -linear * (1.0 + SKALAK_HARDEN * stretch / (1.0 + stretch))


def parts3(a):
    first = a.astype(jnp.bfloat16).astype(jnp.float32)
    rest = a - first
    second = rest.astype(jnp.bfloat16).astype(jnp.float32)
    return first, second, rest - second


def stack_left(a):
    first, second, third = parts3(a)
    return jnp.concatenate([first, first, first, second, second, third], axis=0)


def stack_right(a):
    first, second, third = parts3(a)
    return jnp.concatenate([first, second, third, first, second, first], axis=0)


def stack_pair(a):
    first, second, _ = parts3(a)
    return jnp.concatenate([first, second], axis=0).astype(jnp.bfloat16)


def rows8(rows):
    size = rows[0].shape[1]
    count = sum(row.shape[0] for row in rows)
    return jnp.concatenate(rows + [jnp.zeros((SUB - count, size), jnp.float32)], axis=0)


def square_of(place):
    return jnp.sum(place * place, axis=0, keepdims=True)


def target_rows(place):
    return rows8([place, square_of(place), jnp.ones_like(place[:1])])


def source_rows(place, force):
    near = rows8(
        [-2.0 * place, jnp.ones_like(place[:1]), square_of(place) + EPSILON_SQ]
    )
    along = rows8(
        [
            force,
            jnp.zeros_like(place[:1]),
            -jnp.sum(place * force, axis=0, keepdims=True),
        ]
    )
    return near, along


def weights(shifted, along):
    root = lax.rsqrt(jnp.maximum(shifted, EPSILON_SQ))
    inverse = root * root * root
    return split(root + EPSILON_SQ * inverse) + split(along * inverse)


def twice(a):
    return jnp.concatenate([a, a], axis=1)


def finish(place, direct, moment):
    direct = direct[:SUB] + direct[SUB:]
    moment = moment[:SUB] + moment[SUB:]
    return VISCOSITY * (direct[0:3] + place * moment[3:4] - moment[0:3])


def membrane_kernel(points_ref, rest_ref, up_ref, *refs, fresh):
    count = 1 if fresh else 2
    stiffness_refs, out_ref = refs[:count], refs[count]
    split_refs, (rows_ref, flat_ref) = refs[count + 1 : -2], refs[-2:]
    cells, size = points_ref.shape[1:]
    q = up_ref.shape[0]
    tail = q - LANES
    rows_ref[...] = jnp.zeros_like(rows_ref)
    centers = []
    for k in range(3):
        own = points_ref[k]
        mean = jnp.mean(own, axis=1, keepdims=True)
        rows_ref[SUB * k : SUB * k + cells, :] = own - mean - rest_ref[k : k + 1, :]
        centers.append(jnp.mean(mean, axis=0, keepdims=True))
    if len(stiffness_refs) == 1:
        stiffness = split(stiffness_refs[0][...])
        for ref, part in zip(split_refs, stiffness):
            ref[...] = part
    else:
        stiffness = [ref[...] for ref in stiffness_refs]
    linear = dot3(rows_ref[...], stiffness)
    parts = [linear[SUB * k : SUB * (k + 1)] for k in range(3)]
    stretch = parts[0] * parts[0] + parts[1] * parts[1] + parts[2] * parts[2]
    sums = [jnp.sum(harden(part, stretch), axis=0, keepdims=True) for part in parts]
    summed = jnp.concatenate(sums + [jnp.zeros((SUB - 3, size), jnp.float32)], axis=0)
    flat_ref[...] = jnp.zeros_like(flat_ref)
    flat_ref[:, :q] = dot3(summed, split(up_ref[...]), NT)
    ends = flat_ref[:, LANES:]
    last = ends[0:1]
    lane = lax.broadcasted_iota(jnp.int32, (1, LANES), 1)
    for k in range(1, 3):
        last = last + pltpu.roll(ends[k : k + 1], tail * k, axis=1)
    for k in range(3):
        last = jnp.where(lane == 3 * tail + k, centers[k], last)
    message = jnp.concatenate([flat_ref[0:3, :LANES], last], axis=0)
    out_ref[...] = jnp.broadcast_to(message[None], out_ref.shape)


def pick(block, row):
    rows = lax.broadcasted_iota(jnp.int32, (block.shape[0], 1), 0)
    return jnp.sum(jnp.where(rows == row, block, 0.0), axis=0, keepdims=True)


def near_kernel(
    target_ref,
    owner_ref,
    cell_ref,
    count_ref,
    own_ref,
    *refs,
    spread,
):
    pool_refs, (rest_ref, high_ref, low_ref, out_ref, rows_ref, move_ref) = (
        refs[:-6],
        refs[-6:],
    )
    size = own_ref.shape[2]
    me = lax.axis_index("dev")
    rows_ref[...] = jnp.zeros_like(rows_ref)
    move_ref[...] = jnp.zeros_like(move_ref)
    for slot in range(NEAR):
        cell = cell_ref[0, slot]
        owner = owner_ref[0, slot]
        if spread:
            for mask, pool_ref in enumerate(pool_refs):

                @pl.when((owner ^ me) == mask)
                def _(pool_ref=pool_ref):
                    for k in range(3):
                        rows_ref[SUB * slot + k : SUB * slot + k + 1, :] = pick(pool_ref[k], cell)
        else:
            for k in range(3):
                rows_ref[SUB * slot + k : SUB * slot + k + 1, :] = pick(
                    pool_refs[0][owner, k], cell
                )
    sources = rows_ref[...]
    for slot in range(NEAR):
        own = sources[SUB * slot : SUB * slot + 3]
        mean = jnp.mean(own, axis=1, keepdims=True)
        move_ref[SUB * slot : SUB * slot + 3, :] = own - mean - rest_ref[...]
    linear = dot3(move_ref[...], (high_ref[...], low_ref[...]))
    square = linear * linear
    for slot in range(NEAR):
        part = linear[SUB * slot : SUB * slot + 3]
        stretch = jnp.sum(square[SUB * slot : SUB * slot + 3], axis=0, keepdims=True)
        rows_ref[SUB * slot + 3 : SUB * slot + 6, :] = harden(part, stretch)
    dot = functools.partial(jnp.dot, preferred_element_type=jnp.float32)
    results = []
    for slot in range(NEAR):
        aim = jnp.concatenate([pick(own_ref[k], target_ref[0, slot]) for k in range(3)], axis=0)
        center = jnp.mean(aim, axis=1, keepdims=True)
        aim = aim - center
        place = rows_ref[SUB * slot : SUB * slot + 3, :] - center
        force = rows_ref[SUB * slot + 3 : SUB * slot + 6, :]
        near, along = source_rows(place, force)
        near = jnp.transpose(stack_left(near)).astype(jnp.bfloat16)
        along = jnp.transpose(stack_left(along)).astype(jnp.bfloat16)
        right = stack_right(target_rows(aim)).astype(jnp.bfloat16)
        forces = stack_pair(rows8([force]))
        places = stack_pair(rows8([place, jnp.ones_like(place[:1])]))
        direct = jnp.zeros((2 * SUB, size), jnp.float32)
        moment = direct
        for row in range(0, size, CHUNK):
            part = slice(row, min(row + CHUNK, size))
            both = weights(dot(near[part], right), dot(along[part], right))
            direct += dot(twice(forces[:, part]), jnp.concatenate(both[:2], axis=0))
            moment += dot(twice(places[:, part]), jnp.concatenate(both[2:], axis=0))
        results.append(jnp.where(slot < count_ref[0], finish(aim, direct, moment), 0.0))
    cells = lax.broadcasted_iota(jnp.int32, (out_ref.shape[1], 1), 0)
    for k in range(3):
        out_ref[k] = sum(
            jnp.where(cells == target_ref[0, slot], results[slot][k : k + 1], 0.0)
            for slot in range(NEAR)
        )


def boxes(main, ends, center, template, radius, per_row):
    count = main[0].shape[0]
    tail_lanes = template[2]
    rows = []
    for k in range(3):
        place_main = center[k] + radius * template[0][k : k + 1]
        place_ends = jnp.where(tail_lanes, center[k] + radius * template[1][k : k + 1], 0.0)
        rows.append((place_main, place_ends))
    for k in range(3):
        rows.append((main[k], ends[k]))
    packed = []
    for whole, part in rows:
        turn = lax.broadcasted_iota(jnp.int32, (count, 1), 0) % per_row[0]
        shifted = jnp.where(turn == 0, part, 0.0)
        for i in range(1, per_row[0]):
            shifted += jnp.where(turn == i, pltpu.roll(part, per_row[1] * i, axis=1), 0.0)
        packed.append(
            [whole]
            + [
                jnp.sum(shifted[a : min(a + per_row[0], count)], axis=0, keepdims=True)
                for a in range(0, count, per_row[0])
            ]
        )
    return packed


def far_kernel(
    told_ref,
    points_ref,
    near_ref,
    m2m_ref,
    template_ref,
    down_ref,
    points_out_ref,
    velocity_ref,
    wide_ref,
    sums_ref,
    group_ref,
    source_ref,
    *,
    groups,
    devs,
):
    q = template_ref.shape[1]
    tail = q - LANES
    per_row = (LANES // tail, tail)
    group = lax.axis_index("grp")
    dev = lax.axis_index("dev")
    lane = lax.broadcasted_iota(jnp.int32, (1, LANES), 1)
    tail_lanes = lane < tail

    def ends_of(row, k):
        moved = pltpu.roll(row, LANES - tail * k, axis=1) if k else row
        return jnp.where(tail_lanes, moved, 0.0)

    wide_ref[...] = jnp.zeros_like(wide_ref)
    wide_ref[0:3, :q] = template_ref[...]
    template = (wide_ref[:, :LANES], wide_ref[:, LANES:], tail_lanes)

    first = group * devs
    own_rows = [told_ref[pl.ds(first, devs), k, :] for k in range(4)]
    others = lax.broadcasted_iota(jnp.int32, (devs, 1), 0) != dev
    inner = boxes(
        [jnp.where(others, own_rows[k], 0.0) for k in range(3)],
        [jnp.where(others, ends_of(own_rows[3], k), 0.0) for k in range(3)],
        [own_rows[3][:, 3 * tail + k : 3 * tail + k + 1] for k in range(3)],
        template,
        DEVICE_RADIUS,
        per_row,
    )

    span = up8(groups)
    sums_ref[...] = jnp.zeros_like(sums_ref)
    for h in range(groups):
        sums_ref[h] = jnp.sum(told_ref[h * devs : (h + 1) * devs], axis=0)
    sum_rows = [sums_ref[:, k, :] for k in range(4)]
    for k in range(3):
        group_ref[span * k : span * (k + 1), :LANES] = sum_rows[k]
        group_ref[span * k : span * (k + 1), LANES:] = ends_of(sum_rows[3], k)
    shifted = dot3(group_ref[:, :q], split(m2m_ref[...]))
    group_ref[:, :q] = shifted
    other_groups = lax.broadcasted_iota(jnp.int32, (span, 1), 0) != group
    outer = boxes(
        [
            jnp.where(other_groups, group_ref[span * k : span * (k + 1), :LANES], 0.0)
            for k in range(3)
        ],
        [
            jnp.where(other_groups, group_ref[span * k : span * (k + 1), LANES:], 0.0)
            for k in range(3)
        ],
        [sum_rows[3][:, 3 * tail + k : 3 * tail + k + 1] / devs for k in range(3)],
        template,
        GROUP_RADIUS,
        per_row,
    )
    source_ref[...] = jnp.zeros_like(source_ref)
    rows = 0
    center_row = told_ref[pl.ds(first + dev, 1), 3, :]
    centers = [center_row[:, 3 * tail + k : 3 * tail + k + 1] for k in range(3)]
    for part, count in ((inner, devs), (outer, groups)):
        ends = -(-count // per_row[0])
        for index in range(6):
            shift = centers[index] if index < 3 else 0.0
            source_ref[rows : rows + count, index, :] = part[index][0][:count] - shift
            for j in range(ends):
                at = rows + count + j
                source_ref[at : at + 1, index, :] = part[index][1 + j] - shift
        rows += count + ends
    tall = up8(up8(q) // 2) * 2
    targets = CHECK_RADIUS * wide_ref[0:3, :]
    left = jnp.transpose(stack_left(target_rows(targets)))[:tall].astype(jnp.bfloat16)
    targets = targets[:, :tall]
    contract = functools.partial(
        lax.dot_general,
        dimension_numbers=NT,
        preferred_element_type=jnp.float32,
    )
    dot = functools.partial(jnp.dot, preferred_element_type=jnp.float32)
    direct = jnp.zeros((2 * SUB, tall), jnp.float32)
    moment = jnp.zeros((2 * SUB, tall), jnp.float32)
    for row in range(0, source_ref.shape[0], BATCH):
        block = jnp.concatenate([source_ref[row + i] for i in range(BATCH)], axis=1)
        place = block[0:3]
        force = block[3:6]
        near, along = source_rows(place, force)
        both = weights(
            dot(left, stack_right(near).astype(jnp.bfloat16)),
            dot(left, stack_right(along).astype(jnp.bfloat16)),
        )
        forces = stack_pair(rows8([force]))
        places = stack_pair(rows8([place, jnp.ones_like(place[:1])]))
        direct += contract(twice(forces), jnp.concatenate(both[:2], axis=1))
        moment += contract(twice(places), jnp.concatenate(both[2:], axis=1))
    checks = jnp.concatenate(
        [finish(targets, direct, moment)[:, :q], jnp.zeros((SUB - 3, q), jnp.float32)], axis=0
    )
    surface = dot3(checks, split(down_ref[...]))
    for k in range(3):
        velocity = surface[k : k + 1] + near_ref[k]
        velocity_ref[k] = velocity
        points_out_ref[k] = points_ref[k] + TIME_STEP * velocity


PARAMS = pltpu.CompilerParams(vmem_limit_bytes=20 * 2**20)
VMEM = pl.BlockSpec(memory_space=pltpu.VMEM)
SMEM = pl.BlockSpec(memory_space=pltpu.SMEM)


def float32(*shape):
    return jax.ShapeDtypeStruct(shape, jnp.float32)


def body(
    positions,
    rest_shape,
    stiffness,
    up_map,
    down_map,
    m2m,
    box_template,
    near_target,
    near_owner,
    near_cell,
    near_count,
):
    devs = lax.axis_size("dev")
    groups = lax.axis_size("grp")
    cells, size = positions.shape[1:]
    q = up_map.shape[1]
    spread = devs == 8
    span = up8(groups)
    tail_boxes = LANES // (q - LANES)
    source_count = devs + groups + -(-devs // tail_boxes) + -(-groups // tail_boxes)

    def membrane(*args):
        fresh = len(args) == 4
        told = float32(groups * devs, 4, LANES)
        part = jax.ShapeDtypeStruct((size, size), jnp.bfloat16)
        return pl.pallas_call(
            functools.partial(membrane_kernel, fresh=fresh),
            out_shape=(told, part, part) if fresh else (told,),
            in_specs=[VMEM] * len(args),
            out_specs=(VMEM,) * (3 if fresh else 1),
            scratch_shapes=[
                pltpu.VMEM((3 * SUB, size), jnp.float32),
                pltpu.VMEM((SUB, 2 * LANES), jnp.float32),
            ],
            name="membrane",
            compiler_params=PARAMS,
            cost_estimate=pl.CostEstimate(flops=10**9, bytes_accessed=10**6, transcendentals=0),
        )(*args)

    pools = 8 if spread else 1
    near = pl.pallas_call(
        functools.partial(near_kernel, spread=spread),
        out_shape=float32(3, cells, size),
        in_specs=[SMEM] * 4 + [VMEM] * (1 + pools + 3),
        out_specs=VMEM,
        scratch_shapes=[
            pltpu.VMEM((NEAR * SUB, size), jnp.float32),
            pltpu.VMEM((NEAR * SUB, size), jnp.float32),
        ],
        name="near",
        compiler_params=PARAMS,
        cost_estimate=pl.CostEstimate(flops=4 * 10**9, bytes_accessed=10**6, transcendentals=0),
    )
    far = pl.pallas_call(
        functools.partial(far_kernel, groups=groups, devs=devs),
        out_shape=(float32(3, cells, size), float32(3, cells, size)),
        in_specs=[VMEM] * 6,
        out_specs=(VMEM, VMEM),
        scratch_shapes=[
            pltpu.VMEM((SUB, 2 * LANES), jnp.float32),
            pltpu.VMEM((span, 4, LANES), jnp.float32),
            pltpu.VMEM((3 * span, 2 * LANES), jnp.float32),
            pltpu.VMEM((-(-source_count // BATCH) * BATCH, SUB, LANES), jnp.float32),
        ],
        name="far",
        compiler_params=PARAMS,
        cost_estimate=pl.CostEstimate(flops=2 * 10**9, bytes_accessed=10**6, transcendentals=0),
    )

    def to(array, mask):
        return lax.ppermute(array, "dev", [(j, j ^ mask) for j in range(devs)])

    points = positions
    velocity = None
    parts = [stiffness]
    for _ in range(STEPS):
        message, *fresh = membrane(points, rest_shape, up_map.T, *parts)
        parts = fresh or parts
        told = lax.all_to_all(message, ("grp", "dev"), 0, 0)
        if spread:
            pool = [to(points, 6)]
            pool = [points] + [to(points, mask) for mask in (2, 4)] + pool
            twins = [to(points, 1)]
            twins += [to(array, 1) for array in pool[1:]]
            pool = [(pool, twins)[mask % 2][mask // 2] for mask in range(8)]
        else:
            copies = jnp.broadcast_to(points[None], (devs,) + points.shape)
            pool = [lax.all_to_all(copies, "dev", 0, 0)]
        close = near(
            near_target,
            near_owner,
            near_cell,
            near_count,
            points,
            *pool,
            rest_shape,
            *parts,
        )
        points, velocity = far(told, points, close, m2m, box_template, down_map)
    return (points, velocity)


def solution(mesh):
    both = ("grp", "dev")
    return jax.shard_map(
        body,
        mesh=mesh,
        in_specs=(P(None, both, None),) + (P(),) * 6 + (P(both, None),) * 3 + (P(both),),
        out_specs=(P(None, both, None), P(None, both, None)),
        check_vma=False,
    )
```

```python
import functools

import jax
import jax.numpy as jnp
from jax import lax
from jax.experimental import pallas as pl
from jax.experimental.pallas import tpu as pltpu
from jax.sharding import PartitionSpec as P


NEAR = 2

EPSILON_SQ = 0.25
VISCOSITY = 0.039788735772973836
TIME_STEP = 0.1
SKALAK_HARDEN = 2.0
CHECK_RADIUS = 1.0
DEVICE_RADIUS = 1.5
GROUP_RADIUS = 6.0

LANES = 128
SUB = 8
BATCH = 3


def up8(n):
    return -(-n // SUB) * SUB


def split(a):
    high = a.astype(jnp.bfloat16)
    low = (a - high.astype(jnp.float32)).astype(jnp.bfloat16)
    return high, low


NN = (((1,), (0,)), ((), ()))
NT = (((1,), (1,)), ((), ()))


def dot3(a, b_parts, dims=NN):
    dot = functools.partial(
        lax.dot_general, dimension_numbers=dims, preferred_element_type=jnp.float32
    )
    rows = a.shape[0]
    first = a.astype(jnp.bfloat16).astype(jnp.float32)
    both = jnp.concatenate([first, a - first], axis=0).astype(jnp.bfloat16)
    high = dot(both, b_parts[0])
    return high[:rows] + (high[rows:] + dot(first.astype(jnp.bfloat16), b_parts[1]))


def harden(linear, stretch):
    return -linear * (1.0 + SKALAK_HARDEN * stretch / (1.0 + stretch))


def parts3(a):
    first = a.astype(jnp.bfloat16).astype(jnp.float32)
    rest = a - first
    second = rest.astype(jnp.bfloat16).astype(jnp.float32)
    return first, second, rest - second


def stack_left(a):
    first, second, third = parts3(a)
    return jnp.concatenate([first, first, first, second, second, third], axis=0)


def stack_right(a):
    first, second, third = parts3(a)
    return jnp.concatenate([first, second, third, first, second, first], axis=0)


def stack_pair(a):
    first, second, _ = parts3(a)
    return jnp.concatenate([first, second], axis=0).astype(jnp.bfloat16)


def rows8(rows):
    size = rows[0].shape[1]
    count = sum(row.shape[0] for row in rows)
    return jnp.concatenate(rows + [jnp.zeros((SUB - count, size), jnp.float32)], axis=0)


def square_of(place):
    return jnp.sum(place * place, axis=0, keepdims=True)


def target_rows(place):
    return rows8([place, square_of(place), jnp.ones_like(place[:1])])


def source_rows(place, force):
    near = rows8(
        [-2.0 * place, jnp.ones_like(place[:1]), square_of(place) + EPSILON_SQ]
    )
    along = rows8(
        [
            force,
            jnp.zeros_like(place[:1]),
            -jnp.sum(place * force, axis=0, keepdims=True),
        ]
    )
    return near, along


def weights(shifted, along):
    root = lax.rsqrt(jnp.maximum(shifted, EPSILON_SQ))
    inverse = root * root * root
    return split(root + EPSILON_SQ * inverse) + split(along * inverse)


def twice(a):
    return jnp.concatenate([a, a], axis=1)


def finish(place, direct, moment):
    direct = direct[:SUB] + direct[SUB:]
    moment = moment[:SUB] + moment[SUB:]
    return VISCOSITY * (direct[0:3] + place * moment[3:4] - moment[0:3])


def membrane_rows(points, rest_ref, rows_ref):
    cells = points[0].shape[0]
    rows_ref[...] = jnp.zeros_like(rows_ref)
    centers = []
    for k in range(3):
        mean = jnp.mean(points[k], axis=1, keepdims=True)
        rows_ref[SUB * k : SUB * k + cells, :] = points[k] - mean - rest_ref[k : k + 1, :]
        centers.append(jnp.mean(mean, axis=0, keepdims=True))
    return centers


def equivalent_rows(linear, up, flat_ref):
    parts = [linear[SUB * k : SUB * (k + 1)] for k in range(3)]
    stretch = parts[0] * parts[0] + parts[1] * parts[1] + parts[2] * parts[2]
    sums = [jnp.sum(harden(part, stretch), axis=0, keepdims=True) for part in parts]
    flat_ref[...] = jnp.zeros_like(flat_ref)
    flat_ref[:, : up.shape[0]] = dot3(rows8(sums), split(up), NT)


def pack(flat_ref, q, centers=()):
    tail = q - LANES
    ends = flat_ref[:, LANES:]
    last = ends[0:1]
    lane = lax.broadcasted_iota(jnp.int32, (1, LANES), 1)
    for k in range(1, 3):
        last = last + pltpu.roll(ends[k : k + 1], tail * k, axis=1)
    for k, center in enumerate(centers):
        last = jnp.where(lane == 3 * tail + k, center, last)
    return jnp.concatenate([flat_ref[0:3, :LANES], last], axis=0)


def ends_of(row, k, tail):
    lane = lax.broadcasted_iota(jnp.int32, (1, LANES), 1)
    moved = pltpu.roll(row, LANES - tail * k, axis=1) if k else row
    return jnp.where(lane < tail, moved, 0.0)


def first_kernel(points_ref, rest_ref, up_ref, stiffness_ref, out_ref, rows_ref, flat_ref):
    centers = membrane_rows([points_ref[k] for k in range(3)], rest_ref, rows_ref)
    linear = dot3(rows_ref[...], split(stiffness_ref[...]))
    equivalent_rows(linear, up_ref[...], flat_ref)
    message = pack(flat_ref, up_ref.shape[0], centers)
    out_ref[...] = jnp.broadcast_to(message[None], out_ref.shape)


def pick(block, row):
    rows = lax.broadcasted_iota(jnp.int32, (block.shape[0], 1), 0)
    return jnp.sum(jnp.where(rows == row, block, 0.0), axis=0, keepdims=True)


def gather(owner_ref, cell_ref, pool_refs, rows_ref, spread):
    me = lax.axis_index("dev")
    rows_ref[...] = jnp.zeros_like(rows_ref)
    for slot in range(NEAR):
        cell = cell_ref[0, slot]
        owner = owner_ref[0, slot]
        if spread:
            for mask, pool_ref in enumerate(pool_refs):

                @pl.when((owner ^ me) == mask)
                def _(pool_ref=pool_ref):
                    for k in range(3):
                        rows_ref[SUB * slot + k : SUB * slot + k + 1, :] = pick(pool_ref[k], cell)
        else:
            for k in range(3):
                rows_ref[SUB * slot + k : SUB * slot + k + 1, :] = pick(
                    pool_refs[0][owner, k], cell
                )


def near_sums(target_ref, count_ref, points_ref, rest_ref, stiffness, rows_ref, move_ref):
    cells, _ = points_ref.shape[1:]
    sources = rows_ref[...]
    move_ref[...] = jnp.zeros_like(move_ref)
    for slot in range(NEAR):
        own = sources[SUB * slot : SUB * slot + 3]
        mean = jnp.mean(own, axis=1, keepdims=True)
        move_ref[SUB * slot : SUB * slot + 3, :] = own - mean - rest_ref[...]
    linear = dot3(move_ref[...], stiffness)
    square = linear * linear
    dot = functools.partial(jnp.dot, preferred_element_type=jnp.float32)
    results = []
    for slot in range(NEAR):
        part = linear[SUB * slot : SUB * slot + 3]
        stretch = jnp.sum(square[SUB * slot : SUB * slot + 3], axis=0, keepdims=True)
        force = harden(part, stretch)
        aim = jnp.concatenate([pick(points_ref[k], target_ref[0, slot]) for k in range(3)], axis=0)
        center = jnp.mean(aim, axis=1, keepdims=True)
        aim = aim - center
        place = sources[SUB * slot : SUB * slot + 3] - center
        near, along = source_rows(place, force)
        near = jnp.transpose(stack_left(near)).astype(jnp.bfloat16)
        along = jnp.transpose(stack_left(along)).astype(jnp.bfloat16)
        right = stack_right(target_rows(aim)).astype(jnp.bfloat16)
        forces = stack_pair(rows8([force]))
        places = stack_pair(rows8([place, jnp.ones_like(place[:1])]))
        both = weights(dot(near, right), dot(along, right))
        direct = dot(twice(forces), jnp.concatenate(both[:2], axis=0))
        moment = dot(twice(places), jnp.concatenate(both[2:], axis=0))
        results.append(jnp.where(slot < count_ref[0], finish(aim, direct, moment), 0.0))
    rows = lax.broadcasted_iota(jnp.int32, (cells, 1), 0)
    return [
        sum(
            jnp.where(rows == target_ref[0, slot], results[slot][k : k + 1], 0.0)
            for slot in range(NEAR)
        )
        for k in range(3)
    ]


def near_kernel(target_ref, owner_ref, cell_ref, count_ref, points_ref, *refs, spread, move):
    pool_refs, (rest_ref, stiffness_ref, out_ref, rows_ref, move_ref) = refs[:-5], refs[-5:]
    gather(owner_ref, cell_ref, pool_refs, rows_ref, spread)
    stiffness = split(stiffness_ref[...])
    near = near_sums(target_ref, count_ref, points_ref, rest_ref, stiffness, rows_ref, move_ref)
    for k in range(3):
        out_ref[k] = points_ref[k] + TIME_STEP * near[k] if move else near[k]


def boxes(main, ends, center, template, radius, per_row):
    count = main[0].shape[0]
    tail_lanes = template[2]
    rows = []
    for k in range(3):
        place_main = center[k] + radius * template[0][k : k + 1]
        place_ends = jnp.where(tail_lanes, center[k] + radius * template[1][k : k + 1], 0.0)
        rows.append((place_main, place_ends))
    for k in range(3):
        rows.append((main[k], ends[k]))
    packed = []
    for whole, part in rows:
        turn = lax.broadcasted_iota(jnp.int32, (count, 1), 0) % per_row[0]
        shifted = jnp.where(turn == 0, part, 0.0)
        for i in range(1, per_row[0]):
            shifted += jnp.where(turn == i, pltpu.roll(part, per_row[1] * i, axis=1), 0.0)
        packed.append(
            [whole]
            + [
                jnp.sum(shifted[a : min(a + per_row[0], count)], axis=0, keepdims=True)
                for a in range(0, count, per_row[0])
            ]
        )
    return packed


def far_checks(
    told_ref, m2m_ref, template_ref, wide_ref, sums_ref, group_ref, source_ref, groups, devs
):
    q = template_ref.shape[1]
    tail = q - LANES
    per_row = (LANES // tail, tail)
    group = lax.axis_index("grp")
    dev = lax.axis_index("dev")
    tail_lanes = lax.broadcasted_iota(jnp.int32, (1, LANES), 1) < tail

    wide_ref[...] = jnp.zeros_like(wide_ref)
    wide_ref[0:3, :q] = template_ref[...]
    template = (wide_ref[:, :LANES], wide_ref[:, LANES:], tail_lanes)

    first = group * devs
    own_rows = [told_ref[pl.ds(first, devs), k, :] for k in range(4)]
    others = lax.broadcasted_iota(jnp.int32, (devs, 1), 0) != dev
    inner = boxes(
        [jnp.where(others, own_rows[k], 0.0) for k in range(3)],
        [jnp.where(others, ends_of(own_rows[3], k, tail), 0.0) for k in range(3)],
        [own_rows[3][:, 3 * tail + k : 3 * tail + k + 1] for k in range(3)],
        template,
        DEVICE_RADIUS,
        per_row,
    )

    span = up8(groups)
    sums_ref[...] = jnp.zeros_like(sums_ref)
    for h in range(groups):
        sums_ref[h] = jnp.sum(told_ref[h * devs : (h + 1) * devs, 0:4, :], axis=0)
    sum_rows = [sums_ref[:, k, :] for k in range(4)]
    for k in range(3):
        group_ref[span * k : span * (k + 1), :LANES] = sum_rows[k]
        group_ref[span * k : span * (k + 1), LANES:] = ends_of(sum_rows[3], k, tail)
    shifted = dot3(group_ref[:, :q], split(m2m_ref[...]))
    group_ref[:, :q] = shifted
    other_groups = lax.broadcasted_iota(jnp.int32, (span, 1), 0) != group
    outer = boxes(
        [
            jnp.where(other_groups, group_ref[span * k : span * (k + 1), :LANES], 0.0)
            for k in range(3)
        ],
        [
            jnp.where(other_groups, group_ref[span * k : span * (k + 1), LANES:], 0.0)
            for k in range(3)
        ],
        [sum_rows[3][:, 3 * tail + k : 3 * tail + k + 1] / devs for k in range(3)],
        template,
        GROUP_RADIUS,
        per_row,
    )
    source_ref[...] = jnp.zeros_like(source_ref)
    rows = 0
    center_row = told_ref[pl.ds(first + dev, 1), 3, :]
    centers = [center_row[:, 3 * tail + k : 3 * tail + k + 1] for k in range(3)]
    for part, count in ((inner, devs), (outer, groups)):
        ends = -(-count // per_row[0])
        for index in range(6):
            shift = centers[index] if index < 3 else 0.0
            source_ref[rows : rows + count, index, :] = part[index][0][:count] - shift
            for j in range(ends):
                at = rows + count + j
                source_ref[at : at + 1, index, :] = part[index][1 + j] - shift
        rows += count + ends
    tall = up8(up8(q) // 2) * 2
    targets = CHECK_RADIUS * wide_ref[0:3, :]
    left = jnp.transpose(stack_left(target_rows(targets)))[:tall].astype(jnp.bfloat16)
    targets = targets[:, :tall]
    contract = functools.partial(
        lax.dot_general,
        dimension_numbers=NT,
        preferred_element_type=jnp.float32,
    )
    dot = functools.partial(jnp.dot, preferred_element_type=jnp.float32)
    direct = jnp.zeros((2 * SUB, tall), jnp.float32)
    moment = jnp.zeros((2 * SUB, tall), jnp.float32)
    for row in range(0, source_ref.shape[0], BATCH):
        block = jnp.concatenate([source_ref[row + i] for i in range(BATCH)], axis=1)
        place = block[0:3]
        force = block[3:6]
        near, along = source_rows(place, force)
        both = weights(
            dot(left, stack_right(near).astype(jnp.bfloat16)),
            dot(left, stack_right(along).astype(jnp.bfloat16)),
        )
        forces = stack_pair(rows8([force]))
        places = stack_pair(rows8([place, jnp.ones_like(place[:1])]))
        direct += contract(twice(forces), jnp.concatenate(both[:2], axis=1))
        moment += contract(twice(places), jnp.concatenate(both[2:], axis=1))
    return finish(targets, direct, moment)[:, :q]


def surface_of(checks, down_ref):
    return dot3(rows8([checks]), split(down_ref[...]))


def turn_kernel(
    told_ref,
    partial_ref,
    m2m_ref,
    template_ref,
    down_ref,
    rest_ref,
    up_ref,
    stiffness_ref,
    points_ref,
    out_ref,
    *refs,
    groups,
    devs,
):
    rows_ref, flat_ref = refs[-2:]
    checks = far_checks(told_ref, m2m_ref, template_ref, *refs[:-2], groups, devs)
    surface = surface_of(checks, down_ref)
    points = [partial_ref[k] + TIME_STEP * surface[k : k + 1] for k in range(3)]
    for k in range(3):
        points_ref[k] = points[k]
    centers = membrane_rows(points, rest_ref, rows_ref)
    linear = dot3(rows_ref[...], split(stiffness_ref[...]))
    equivalent_rows(linear, up_ref[...], flat_ref)
    message = pack(flat_ref, up_ref.shape[0], centers)
    out_ref[...] = jnp.broadcast_to(message[None], out_ref.shape)


def last_kernel(
    told_ref,
    points_ref,
    near_ref,
    m2m_ref,
    template_ref,
    down_ref,
    points_out_ref,
    velocity_ref,
    *refs,
    groups,
    devs,
):
    checks = far_checks(told_ref, m2m_ref, template_ref, *refs, groups, devs)
    surface = surface_of(checks, down_ref)
    for k in range(3):
        velocity = surface[k : k + 1] + near_ref[k]
        velocity_ref[k] = velocity
        points_out_ref[k] = points_ref[k] + TIME_STEP * velocity


VMEM = pl.BlockSpec(memory_space=pltpu.VMEM)
SMEM = pl.BlockSpec(memory_space=pltpu.SMEM)


def float32(*shape):
    return jax.ShapeDtypeStruct(shape, jnp.float32)


def scratch(*shape):
    return pltpu.VMEM(shape, jnp.float32)


def call(kernel, in_specs, outs, scratch_shapes, gflop, mib=24):
    return pl.pallas_call(
        kernel,
        in_specs=in_specs,
        out_shape=tuple(outs),
        out_specs=(VMEM,) * len(outs),
        scratch_shapes=scratch_shapes,
        compiler_params=pltpu.CompilerParams(vmem_limit_bytes=mib * 2**20),
        cost_estimate=pl.CostEstimate(
            flops=gflop * 10**9, bytes_accessed=10**6, transcendentals=0
        ),
    )


def body(
    positions,
    rest_shape,
    stiffness,
    up_map,
    down_map,
    m2m,
    box_template,
    near_target,
    near_owner,
    near_cell,
    near_count,
):
    devs = lax.axis_size("dev")
    groups = lax.axis_size("grp")
    everyone = groups * devs
    cells, size = positions.shape[1:]
    q = up_map.shape[1]
    spread = devs == 8
    pools = 8 if spread else 1
    span = up8(groups)
    tail_boxes = LANES // (q - LANES)
    source_count = devs + groups + -(-devs // tail_boxes) + -(-groups // tail_boxes)
    cell_array = float32(3, cells, size)
    up_rows = up_map.T
    lists = (near_target, near_owner, near_cell, near_count)
    far_scratch = [
        scratch(SUB, 2 * LANES),
        scratch(span, 4, LANES),
        scratch(3 * span, 2 * LANES),
        scratch(-(-source_count // BATCH) * BATCH, SUB, LANES),
    ]
    near_scratch = [scratch(NEAR * SUB, size), scratch(NEAR * SUB, size)]
    membrane_scratch = [scratch(3 * SUB, size), scratch(SUB, 2 * LANES)]

    first = call(
        first_kernel, [VMEM] * 4, [float32(everyone, 4, LANES)], membrane_scratch, 1, mib=62
    )

    def near(points, pool, move):
        kernel = functools.partial(near_kernel, spread=spread, move=move)
        specs = [SMEM] * 4 + [VMEM] * (1 + pools + 2)
        run = call(kernel, specs, [cell_array], near_scratch, 4)
        return run(*lists, points, *pool, rest_shape, stiffness)[0]

    turn = call(
        functools.partial(turn_kernel, groups=groups, devs=devs),
        [VMEM] * 8,
        [cell_array, float32(everyone, 4, LANES)],
        far_scratch + membrane_scratch,
        3,
    )
    last = call(
        functools.partial(last_kernel, groups=groups, devs=devs),
        [VMEM] * 6,
        [cell_array, cell_array],
        far_scratch,
        3,
    )

    def to(array, mask):
        return lax.ppermute(array, "dev", [(j, j ^ mask) for j in range(devs)])

    def pool_of(array):
        if not spread:
            copies = jnp.broadcast_to(array[None], (devs,) + array.shape)
            return [lax.all_to_all(copies, "dev", 0, 0)]
        reached = {0: array}
        for mask in (6, 4, 2):
            reached[mask] = to(array, mask)
        reached[1] = to(array, 1)
        for mask in (2, 4, 6):
            reached[mask + 1] = to(reached[mask], 1)
        return [reached[mask] for mask in range(8)]

    def tell(message):
        return lax.all_to_all(message, ("grp", "dev"), 0, 0)

    pool = pool_of(positions)
    (message,) = first(positions, rest_shape, up_rows, stiffness)
    told = tell(message)
    partial = near(positions, pool, True)
    points, message = turn(
        told, partial, m2m, box_template, down_map, rest_shape, up_rows, stiffness
    )
    pool = pool_of(points)
    told = tell(message)
    close = near(points, pool, False)
    return last(told, points, close, m2m, box_template, down_map)


def solution(mesh):
    both = ("grp", "dev")
    return jax.shard_map(
        body,
        mesh=mesh,
        in_specs=(P(None, both, None),) + (P(),) * 6 + (P(both, None),) * 3 + (P(both),),
        out_specs=(P(None, both, None), P(None, both, None)),
        check_vma=False,
    )
```

```python
import functools

import jax
import jax.numpy as jnp
from jax import lax
from jax.experimental import pallas as pl
from jax.experimental.pallas import tpu as pltpu
from jax.sharding import PartitionSpec as P


NEAR = 2

EPSILON_SQ = 0.25
VISCOSITY = 0.039788735772973836
TIME_STEP = 0.1
SKALAK_HARDEN = 2.0
CHECK_RADIUS = 1.0
DEVICE_RADIUS = 1.5
GROUP_RADIUS = 6.0

LANES = 128
SUB = 8
BATCH = 3


def up8(n):
    return -(-n // SUB) * SUB


def split(a):
    high = a.astype(jnp.bfloat16)
    low = (a - high.astype(jnp.float32)).astype(jnp.bfloat16)
    return high, low


NN = (((1,), (0,)), ((), ()))
NT = (((1,), (1,)), ((), ()))


def dot3(a, b_parts, dims=NN):
    dot = functools.partial(
        lax.dot_general, dimension_numbers=dims, preferred_element_type=jnp.float32
    )
    rows = a.shape[0]
    first = a.astype(jnp.bfloat16).astype(jnp.float32)
    both = jnp.concatenate([first, a - first], axis=0).astype(jnp.bfloat16)
    high = dot(both, b_parts[0])
    return high[:rows] + (high[rows:] + dot(first.astype(jnp.bfloat16), b_parts[1]))


def harden(linear, stretch):
    return -linear * (1.0 + SKALAK_HARDEN * stretch / (1.0 + stretch))


def parts3(a):
    first = a.astype(jnp.bfloat16).astype(jnp.float32)
    rest = a - first
    second = rest.astype(jnp.bfloat16).astype(jnp.float32)
    return first, second, rest - second


def stack_left(a):
    first, second, third = parts3(a)
    return jnp.concatenate([first, first, first, second, second, third], axis=0)


def stack_right(a):
    first, second, third = parts3(a)
    return jnp.concatenate([first, second, third, first, second, first], axis=0)


def stack_pair(a):
    first, second, _ = parts3(a)
    return jnp.concatenate([first, second], axis=0).astype(jnp.bfloat16)


def rows8(rows):
    size = rows[0].shape[1]
    count = sum(row.shape[0] for row in rows)
    return jnp.concatenate(rows + [jnp.zeros((SUB - count, size), jnp.float32)], axis=0)


def square_of(place):
    return jnp.sum(place * place, axis=0, keepdims=True)


def target_rows(place):
    return rows8([place, square_of(place), jnp.ones_like(place[:1])])


def source_rows(place, force):
    near = rows8(
        [-2.0 * place, jnp.ones_like(place[:1]), square_of(place) + EPSILON_SQ]
    )
    along = rows8(
        [
            force,
            jnp.zeros_like(place[:1]),
            -jnp.sum(place * force, axis=0, keepdims=True),
        ]
    )
    return near, along


def weights(shifted, along):
    root = lax.rsqrt(jnp.maximum(shifted, EPSILON_SQ))
    inverse = root * root * root
    return split(root + EPSILON_SQ * inverse) + split(along * inverse)


def twice(a):
    return jnp.concatenate([a, a], axis=1)


def finish(place, direct, moment):
    direct = direct[:SUB] + direct[SUB:]
    moment = moment[:SUB] + moment[SUB:]
    return VISCOSITY * (direct[0:3] + place * moment[3:4] - moment[0:3])


def membrane_rows(points, rest_ref, rows_ref):
    cells = points[0].shape[0]
    rows_ref[...] = jnp.zeros_like(rows_ref)
    centers = []
    for k in range(3):
        mean = jnp.mean(points[k], axis=1, keepdims=True)
        rows_ref[SUB * k : SUB * k + cells, :] = points[k] - mean - rest_ref[k : k + 1, :]
        centers.append(jnp.mean(mean, axis=0, keepdims=True))
    return centers


def equivalent_rows(linear, up, flat_ref):
    parts = [linear[SUB * k : SUB * (k + 1)] for k in range(3)]
    stretch = parts[0] * parts[0] + parts[1] * parts[1] + parts[2] * parts[2]
    sums = [jnp.sum(harden(part, stretch), axis=0, keepdims=True) for part in parts]
    flat_ref[...] = jnp.zeros_like(flat_ref)
    flat_ref[:, : up.shape[0]] = dot3(rows8(sums), split(up), NT)


def pack(flat_ref, q, centers=()):
    tail = q - LANES
    ends = flat_ref[:, LANES:]
    last = ends[0:1]
    lane = lax.broadcasted_iota(jnp.int32, (1, LANES), 1)
    for k in range(1, 3):
        last = last + pltpu.roll(ends[k : k + 1], tail * k, axis=1)
    for k, center in enumerate(centers):
        last = jnp.where(lane == 3 * tail + k, center, last)
    return jnp.concatenate([flat_ref[0:3, :LANES], last], axis=0)


def ends_of(row, k, tail):
    lane = lax.broadcasted_iota(jnp.int32, (1, LANES), 1)
    moved = pltpu.roll(row, LANES - tail * k, axis=1) if k else row
    return jnp.where(lane < tail, moved, 0.0)


def blank_kernel(out_ref):
    out_ref[...] = jnp.zeros_like(out_ref)


def first_kernel(
    blank_ref, points_ref, rest_ref, up_ref, stiffness_ref, out_ref, rows_ref, flat_ref
):
    centers = membrane_rows([points_ref[k] for k in range(3)], rest_ref, rows_ref)
    linear = dot3(rows_ref[...], split(stiffness_ref[...]))
    equivalent_rows(linear, up_ref[...], flat_ref)
    message = pack(flat_ref, up_ref.shape[0], centers) + blank_ref[0:4, :]
    out_ref[...] = jnp.broadcast_to(message[None], out_ref.shape)


def pick(block, row):
    rows = lax.broadcasted_iota(jnp.int32, (block.shape[0], 1), 0)
    return jnp.sum(jnp.where(rows == row, block, 0.0), axis=0, keepdims=True)


def gather(owner_ref, cell_ref, pool_refs, rows_ref, spread):
    me = lax.axis_index("dev")
    rows_ref[...] = jnp.zeros_like(rows_ref)
    for slot in range(NEAR):
        cell = cell_ref[0, slot]
        owner = owner_ref[0, slot]
        if spread:
            for mask, pool_ref in enumerate(pool_refs):

                @pl.when((owner ^ me) == mask)
                def _(pool_ref=pool_ref):
                    for k in range(3):
                        rows_ref[SUB * slot + k : SUB * slot + k + 1, :] = pick(pool_ref[k], cell)
        else:
            for k in range(3):
                rows_ref[SUB * slot + k : SUB * slot + k + 1, :] = pick(
                    pool_refs[0][owner, k], cell
                )


def near_sums(target_ref, count_ref, points_ref, rest_ref, stiffness, rows_ref, move_ref):
    cells, _ = points_ref.shape[1:]
    sources = rows_ref[...]
    move_ref[...] = jnp.zeros_like(move_ref)
    for slot in range(NEAR):
        own = sources[SUB * slot : SUB * slot + 3]
        mean = jnp.mean(own, axis=1, keepdims=True)
        move_ref[SUB * slot : SUB * slot + 3, :] = own - mean - rest_ref[...]
    linear = dot3(move_ref[...], stiffness)
    square = linear * linear
    dot = functools.partial(jnp.dot, preferred_element_type=jnp.float32)
    results = []
    for slot in range(NEAR):
        part = linear[SUB * slot : SUB * slot + 3]
        stretch = jnp.sum(square[SUB * slot : SUB * slot + 3], axis=0, keepdims=True)
        force = harden(part, stretch)
        aim = jnp.concatenate([pick(points_ref[k], target_ref[0, slot]) for k in range(3)], axis=0)
        center = jnp.mean(aim, axis=1, keepdims=True)
        aim = aim - center
        place = sources[SUB * slot : SUB * slot + 3] - center
        near, along = source_rows(place, force)
        near = jnp.transpose(stack_left(near)).astype(jnp.bfloat16)
        along = jnp.transpose(stack_left(along)).astype(jnp.bfloat16)
        right = stack_right(target_rows(aim)).astype(jnp.bfloat16)
        forces = stack_pair(rows8([force]))
        places = stack_pair(rows8([place, jnp.ones_like(place[:1])]))
        both = weights(dot(near, right), dot(along, right))
        direct = dot(twice(forces), jnp.concatenate(both[:2], axis=0))
        moment = dot(twice(places), jnp.concatenate(both[2:], axis=0))
        results.append(jnp.where(slot < count_ref[0], finish(aim, direct, moment), 0.0))
    rows = lax.broadcasted_iota(jnp.int32, (cells, 1), 0)
    return [
        sum(
            jnp.where(rows == target_ref[0, slot], results[slot][k : k + 1], 0.0)
            for slot in range(NEAR)
        )
        for k in range(3)
    ]


def near_kernel(target_ref, owner_ref, cell_ref, count_ref, points_ref, *refs, spread, move):
    pool_refs, (rest_ref, stiffness_ref, out_ref, rows_ref, move_ref) = refs[:-5], refs[-5:]
    gather(owner_ref, cell_ref, pool_refs, rows_ref, spread)
    stiffness = split(stiffness_ref[...])
    near = near_sums(target_ref, count_ref, points_ref, rest_ref, stiffness, rows_ref, move_ref)
    for k in range(3):
        out_ref[k] = points_ref[k] + TIME_STEP * near[k] if move else near[k]


def boxes(main, ends, center, template, radius, per_row):
    count = main[0].shape[0]
    tail_lanes = template[2]
    rows = []
    for k in range(3):
        place_main = center[k] + radius * template[0][k : k + 1]
        place_ends = jnp.where(tail_lanes, center[k] + radius * template[1][k : k + 1], 0.0)
        rows.append((place_main, place_ends))
    for k in range(3):
        rows.append((main[k], ends[k]))
    packed = []
    for whole, part in rows:
        turn = lax.broadcasted_iota(jnp.int32, (count, 1), 0) % per_row[0]
        shifted = jnp.where(turn == 0, part, 0.0)
        for i in range(1, per_row[0]):
            shifted += jnp.where(turn == i, pltpu.roll(part, per_row[1] * i, axis=1), 0.0)
        packed.append(
            [whole]
            + [
                jnp.sum(shifted[a : min(a + per_row[0], count)], axis=0, keepdims=True)
                for a in range(0, count, per_row[0])
            ]
        )
    return packed


def far_checks(
    told_ref, m2m_ref, template_ref, wide_ref, sums_ref, group_ref, source_ref, groups, devs
):
    q = template_ref.shape[1]
    tail = q - LANES
    per_row = (LANES // tail, tail)
    group = lax.axis_index("grp")
    dev = lax.axis_index("dev")
    tail_lanes = lax.broadcasted_iota(jnp.int32, (1, LANES), 1) < tail

    wide_ref[...] = jnp.zeros_like(wide_ref)
    wide_ref[0:3, :q] = template_ref[...]
    template = (wide_ref[:, :LANES], wide_ref[:, LANES:], tail_lanes)

    first = group * devs
    own_rows = [told_ref[pl.ds(first, devs), k, :] for k in range(4)]
    others = lax.broadcasted_iota(jnp.int32, (devs, 1), 0) != dev
    inner = boxes(
        [jnp.where(others, own_rows[k], 0.0) for k in range(3)],
        [jnp.where(others, ends_of(own_rows[3], k, tail), 0.0) for k in range(3)],
        [own_rows[3][:, 3 * tail + k : 3 * tail + k + 1] for k in range(3)],
        template,
        DEVICE_RADIUS,
        per_row,
    )

    span = up8(groups)
    sums_ref[...] = jnp.zeros_like(sums_ref)
    for h in range(groups):
        sums_ref[h] = jnp.sum(told_ref[h * devs : (h + 1) * devs, 0:4, :], axis=0)
    sum_rows = [sums_ref[:, k, :] for k in range(4)]
    for k in range(3):
        group_ref[span * k : span * (k + 1), :LANES] = sum_rows[k]
        group_ref[span * k : span * (k + 1), LANES:] = ends_of(sum_rows[3], k, tail)
    shifted = dot3(group_ref[:, :q], split(m2m_ref[...]))
    group_ref[:, :q] = shifted
    other_groups = lax.broadcasted_iota(jnp.int32, (span, 1), 0) != group
    outer = boxes(
        [
            jnp.where(other_groups, group_ref[span * k : span * (k + 1), :LANES], 0.0)
            for k in range(3)
        ],
        [
            jnp.where(other_groups, group_ref[span * k : span * (k + 1), LANES:], 0.0)
            for k in range(3)
        ],
        [sum_rows[3][:, 3 * tail + k : 3 * tail + k + 1] / devs for k in range(3)],
        template,
        GROUP_RADIUS,
        per_row,
    )
    source_ref[...] = jnp.zeros_like(source_ref)
    rows = 0
    center_row = told_ref[pl.ds(first + dev, 1), 3, :]
    centers = [center_row[:, 3 * tail + k : 3 * tail + k + 1] for k in range(3)]
    for part, count in ((inner, devs), (outer, groups)):
        ends = -(-count // per_row[0])
        for index in range(6):
            shift = centers[index] if index < 3 else 0.0
            source_ref[rows : rows + count, index, :] = part[index][0][:count] - shift
            for j in range(ends):
                at = rows + count + j
                source_ref[at : at + 1, index, :] = part[index][1 + j] - shift
        rows += count + ends
    tall = up8(up8(q) // 2) * 2
    targets = CHECK_RADIUS * wide_ref[0:3, :]
    left = jnp.transpose(stack_left(target_rows(targets)))[:tall].astype(jnp.bfloat16)
    targets = targets[:, :tall]
    contract = functools.partial(
        lax.dot_general,
        dimension_numbers=NT,
        preferred_element_type=jnp.float32,
    )
    dot = functools.partial(jnp.dot, preferred_element_type=jnp.float32)
    direct = jnp.zeros((2 * SUB, tall), jnp.float32)
    moment = jnp.zeros((2 * SUB, tall), jnp.float32)
    for row in range(0, source_ref.shape[0], BATCH):
        block = jnp.concatenate([source_ref[row + i] for i in range(BATCH)], axis=1)
        place = block[0:3]
        force = block[3:6]
        near, along = source_rows(place, force)
        both = weights(
            dot(left, stack_right(near).astype(jnp.bfloat16)),
            dot(left, stack_right(along).astype(jnp.bfloat16)),
        )
        forces = stack_pair(rows8([force]))
        places = stack_pair(rows8([place, jnp.ones_like(place[:1])]))
        direct += contract(twice(forces), jnp.concatenate(both[:2], axis=1))
        moment += contract(twice(places), jnp.concatenate(both[2:], axis=1))
    return finish(targets, direct, moment)[:, :q]


def surface_of(checks, down_ref):
    return dot3(rows8([checks]), split(down_ref[...]))


def turn_kernel(
    told_ref,
    partial_ref,
    m2m_ref,
    template_ref,
    down_ref,
    rest_ref,
    up_ref,
    stiffness_ref,
    points_ref,
    out_ref,
    *refs,
    groups,
    devs,
):
    rows_ref, flat_ref = refs[-2:]
    checks = far_checks(told_ref, m2m_ref, template_ref, *refs[:-2], groups, devs)
    surface = surface_of(checks, down_ref)
    points = [partial_ref[k] + TIME_STEP * surface[k : k + 1] for k in range(3)]
    for k in range(3):
        points_ref[k] = points[k]
    centers = membrane_rows(points, rest_ref, rows_ref)
    linear = dot3(rows_ref[...], split(stiffness_ref[...]))
    equivalent_rows(linear, up_ref[...], flat_ref)
    message = pack(flat_ref, up_ref.shape[0], centers)
    out_ref[...] = jnp.broadcast_to(message[None], out_ref.shape)


def last_kernel(
    told_ref,
    points_ref,
    near_ref,
    m2m_ref,
    template_ref,
    down_ref,
    points_out_ref,
    velocity_ref,
    *refs,
    groups,
    devs,
):
    checks = far_checks(told_ref, m2m_ref, template_ref, *refs, groups, devs)
    surface = surface_of(checks, down_ref)
    for k in range(3):
        velocity = surface[k : k + 1] + near_ref[k]
        velocity_ref[k] = velocity
        points_out_ref[k] = points_ref[k] + TIME_STEP * velocity


VMEM = pl.BlockSpec(memory_space=pltpu.VMEM)
SMEM = pl.BlockSpec(memory_space=pltpu.SMEM)


def float32(*shape):
    return jax.ShapeDtypeStruct(shape, jnp.float32)


def scratch(*shape):
    return pltpu.VMEM(shape, jnp.float32)


def call(kernel, in_specs, outs, scratch_shapes, gflop, mib=24):
    return pl.pallas_call(
        kernel,
        in_specs=in_specs,
        out_shape=tuple(outs),
        out_specs=(VMEM,) * len(outs),
        scratch_shapes=scratch_shapes,
        compiler_params=pltpu.CompilerParams(vmem_limit_bytes=mib * 2**20),
        cost_estimate=pl.CostEstimate(
            flops=gflop * 10**9, bytes_accessed=10**6, transcendentals=0
        ),
    )


def body(
    positions,
    rest_shape,
    stiffness,
    up_map,
    down_map,
    m2m,
    box_template,
    near_target,
    near_owner,
    near_cell,
    near_count,
):
    devs = lax.axis_size("dev")
    groups = lax.axis_size("grp")
    everyone = groups * devs
    cells, size = positions.shape[1:]
    q = up_map.shape[1]
    spread = devs == 8
    pools = 8 if spread else 1
    span = up8(groups)
    tail_boxes = LANES // (q - LANES)
    source_count = devs + groups + -(-devs // tail_boxes) + -(-groups // tail_boxes)
    cell_array = float32(3, cells, size)
    up_rows = up_map.T
    lists = (near_target, near_owner, near_cell, near_count)
    far_scratch = [
        scratch(SUB, 2 * LANES),
        scratch(span, 4, LANES),
        scratch(3 * span, 2 * LANES),
        scratch(-(-source_count // BATCH) * BATCH, SUB, LANES),
    ]
    near_scratch = [scratch(NEAR * SUB, size), scratch(NEAR * SUB, size)]
    membrane_scratch = [scratch(3 * SUB, size), scratch(SUB, 2 * LANES)]

    first = call(first_kernel, [VMEM] * 5, [float32(everyone, 4, LANES)], membrane_scratch, 1)
    blank = call(blank_kernel, [], [float32(SUB, LANES)], [], 40)

    def near(points, pool, move):
        kernel = functools.partial(near_kernel, spread=spread, move=move)
        specs = [SMEM] * 4 + [VMEM] * (1 + pools + 2)
        run = call(kernel, specs, [cell_array], near_scratch, 4)
        return run(*lists, points, *pool, rest_shape, stiffness)[0]

    turn = call(
        functools.partial(turn_kernel, groups=groups, devs=devs),
        [VMEM] * 8,
        [cell_array, float32(everyone, 4, LANES)],
        far_scratch + membrane_scratch,
        3,
    )
    last = call(
        functools.partial(last_kernel, groups=groups, devs=devs),
        [VMEM] * 6,
        [cell_array, cell_array],
        far_scratch,
        3,
    )

    def to(array, mask):
        return lax.ppermute(array, "dev", [(j, j ^ mask) for j in range(devs)])

    def pool_of(array):
        if not spread:
            copies = jnp.broadcast_to(array[None], (devs,) + array.shape)
            return [lax.all_to_all(copies, "dev", 0, 0)]
        reached = {0: array}
        for mask in (6, 4, 2):
            reached[mask] = to(array, mask)
        reached[1] = to(array, 1)
        for mask in (2, 4, 6):
            reached[mask + 1] = to(reached[mask], 1)
        return [reached[mask] for mask in range(8)]

    def tell(message):
        return lax.all_to_all(message, ("grp", "dev"), 0, 0)

    (empty,) = blank()
    pool = pool_of(positions)
    (message,) = first(empty, positions, rest_shape, up_rows, stiffness)
    told = tell(message)
    partial = near(positions, pool, True)
    points, message = turn(
        told, partial, m2m, box_template, down_map, rest_shape, up_rows, stiffness
    )
    pool = pool_of(points)
    told = tell(message)
    close = near(points, pool, False)
    return last(told, points, close, m2m, box_template, down_map)


def solution(mesh):
    both = ("grp", "dev")
    return jax.shard_map(
        body,
        mesh=mesh,
        in_specs=(P(None, both, None),) + (P(),) * 6 + (P(both, None),) * 3 + (P(both),),
        out_specs=(P(None, both, None), P(None, both, None)),
        check_vma=False,
    )
```

```python
import functools

import jax
import jax.numpy as jnp
from jax import lax
from jax.experimental import pallas as pl
from jax.experimental.pallas import tpu as pltpu
from jax.sharding import PartitionSpec as P


NEAR = 2

EPSILON_SQ = 0.25
VISCOSITY = 0.039788735772973836
TIME_STEP = 0.1
SKALAK_HARDEN = 2.0
CHECK_RADIUS = 1.0
DEVICE_RADIUS = 1.5
GROUP_RADIUS = 6.0

LANES = 128
SUB = 8
BATCH = 1
WIDTH = 128
LAG = 1
LEAD = 2


def up8(n):
    return -(-n // SUB) * SUB


def split(a):
    high = a.astype(jnp.bfloat16)
    low = (a - high.astype(jnp.float32)).astype(jnp.bfloat16)
    return high, low


NN = (((1,), (0,)), ((), ()))
NT = (((1,), (1,)), ((), ()))


def dot3(a, b_parts, dims=NN):
    dot = functools.partial(
        lax.dot_general, dimension_numbers=dims, preferred_element_type=jnp.float32
    )
    rows = a.shape[0]
    first = a.astype(jnp.bfloat16).astype(jnp.float32)
    both = jnp.concatenate([first, a - first], axis=0).astype(jnp.bfloat16)
    high = dot(both, b_parts[0])
    return high[:rows] + (high[rows:] + dot(first.astype(jnp.bfloat16), b_parts[1]))


def harden(linear, stretch):
    return -linear * (1.0 + SKALAK_HARDEN * stretch / (1.0 + stretch))


def parts3(a):
    first = a.astype(jnp.bfloat16).astype(jnp.float32)
    rest = a - first
    second = rest.astype(jnp.bfloat16).astype(jnp.float32)
    return first, second, rest - second


def stack_left(a):
    first, second, third = parts3(a)
    return jnp.concatenate([first, first, first, second, second, third], axis=0)


def stack_right(a):
    first, second, third = parts3(a)
    return jnp.concatenate([first, second, third, first, second, first], axis=0)


def stack_pair(a):
    first, second, _ = parts3(a)
    return jnp.concatenate([first, second], axis=0).astype(jnp.bfloat16)


def rows8(rows):
    size = rows[0].shape[1]
    count = sum(row.shape[0] for row in rows)
    return jnp.concatenate(rows + [jnp.zeros((SUB - count, size), jnp.float32)], axis=0)


def square_of(place):
    return jnp.sum(place * place, axis=0, keepdims=True)


def target_rows(place):
    return rows8([place, square_of(place), jnp.ones_like(place[:1])])


def source_rows(place, force):
    near = rows8(
        [-2.0 * place, jnp.ones_like(place[:1]), square_of(place) + EPSILON_SQ]
    )
    along = rows8(
        [
            force,
            jnp.zeros_like(place[:1]),
            -jnp.sum(place * force, axis=0, keepdims=True),
        ]
    )
    return near, along


def weights(shifted, along):
    root = lax.rsqrt(jnp.maximum(shifted, EPSILON_SQ))
    inverse = root * root * root
    return split(root + EPSILON_SQ * inverse) + split(along * inverse)


def twice(a):
    return jnp.concatenate([a, a], axis=1)


def finish(place, direct, moment):
    direct = direct[:SUB] + direct[SUB:]
    moment = moment[:SUB] + moment[SUB:]
    return VISCOSITY * (direct[0:3] + place * moment[3:4] - moment[0:3])


def membrane_rows(points, rest_ref, rows_ref):
    cells = points[0].shape[0]
    rows_ref[...] = jnp.zeros_like(rows_ref)
    centers = []
    for k in range(3):
        mean = jnp.mean(points[k], axis=1, keepdims=True)
        rows_ref[SUB * k : SUB * k + cells, :] = points[k] - mean - rest_ref[k : k + 1, :]
        centers.append(jnp.mean(mean, axis=0, keepdims=True))
    return centers


def equivalent_rows(linear, up, flat_ref):
    parts = [linear[SUB * k : SUB * (k + 1)] for k in range(3)]
    stretch = parts[0] * parts[0] + parts[1] * parts[1] + parts[2] * parts[2]
    sums = [jnp.sum(harden(part, stretch), axis=0, keepdims=True) for part in parts]
    flat_ref[...] = jnp.zeros_like(flat_ref)
    flat_ref[:, : up.shape[0]] = dot3(rows8(sums), split(up), NT)


def pack(flat_ref, q, centers=()):
    tail = q - LANES
    ends = flat_ref[:, LANES:]
    last = ends[0:1]
    lane = lax.broadcasted_iota(jnp.int32, (1, LANES), 1)
    for k in range(1, 3):
        last = last + pltpu.roll(ends[k : k + 1], tail * k, axis=1)
    for k, center in enumerate(centers):
        last = jnp.where(lane == 3 * tail + k, center, last)
    return jnp.concatenate([flat_ref[0:3, :LANES], last], axis=0)


def ends_of(row, k, tail):
    lane = lax.broadcasted_iota(jnp.int32, (1, LANES), 1)
    moved = pltpu.roll(row, LANES - tail * k, axis=1) if k else row
    return jnp.where(lane < tail, moved, 0.0)


def blank_kernel(out_ref):
    out_ref[...] = jnp.zeros_like(out_ref)


def first_kernel(
    blank_ref, points_ref, rest_ref, up_ref, stiffness_ref, out_ref, rows_ref, flat_ref
):
    centers = membrane_rows([points_ref[k] for k in range(3)], rest_ref, rows_ref)
    linear = dot3(rows_ref[...], split(stiffness_ref[...]))
    equivalent_rows(linear, up_ref[...], flat_ref)
    message = pack(flat_ref, up_ref.shape[0], centers) + blank_ref[0:4, :]
    out_ref[...] = jnp.broadcast_to(message[None], out_ref.shape)


def pick(block, row):
    rows = lax.broadcasted_iota(jnp.int32, (block.shape[0], 1), 0)
    return jnp.sum(jnp.where(rows == row, block, 0.0), axis=0, keepdims=True)


def gather(owner_ref, cell_ref, pool_refs, rows_ref, spread):
    me = lax.axis_index("dev")
    rows_ref[...] = jnp.zeros_like(rows_ref)
    for slot in range(NEAR):
        cell = cell_ref[0, slot]
        owner = owner_ref[0, slot]
        if spread:
            for mask, pool_ref in enumerate(pool_refs):

                @pl.when((owner ^ me) == mask)
                def _(pool_ref=pool_ref):
                    for k in range(3):
                        rows_ref[SUB * slot + k : SUB * slot + k + 1, :] = pick(pool_ref[k], cell)
        else:
            for k in range(3):
                rows_ref[SUB * slot + k : SUB * slot + k + 1, :] = pick(
                    pool_refs[0][owner, k], cell
                )


def near_sums(target_ref, count_ref, points_ref, rest_ref, stiffness, rows_ref, move_ref):
    cells, size = points_ref.shape[1:]
    sources = rows_ref[...]
    move_ref[...] = jnp.zeros_like(move_ref)
    for slot in range(NEAR):
        own = sources[SUB * slot : SUB * slot + 3]
        mean = jnp.mean(own, axis=1, keepdims=True)
        move_ref[SUB * slot : SUB * slot + 3, :] = own - mean - rest_ref[...]
    linear = dot3(move_ref[...], stiffness)
    square = linear * linear
    dot = functools.partial(jnp.dot, preferred_element_type=jnp.float32)
    opened = []
    for slot in range(NEAR):
        part = linear[SUB * slot : SUB * slot + 3]
        stretch = jnp.sum(square[SUB * slot : SUB * slot + 3], axis=0, keepdims=True)
        force = harden(part, stretch)
        aim = jnp.concatenate([pick(points_ref[k], target_ref[0, slot]) for k in range(3)], axis=0)
        center = jnp.mean(aim, axis=1, keepdims=True)
        aim = aim - center
        place = sources[SUB * slot : SUB * slot + 3] - center
        near, along = (
            jnp.transpose(stack_left(rows)).astype(jnp.bfloat16)
            for rows in source_rows(place, force)
        )
        right = stack_right(target_rows(aim)).astype(jnp.bfloat16)
        forces = twice(stack_pair(rows8([force])))
        places = twice(stack_pair(rows8([place, jnp.ones_like(place[:1])])))
        for lane in range(0, size, WIDTH):
            part = slice(lane, min(lane + WIDTH, size))
            opened.append((slot, aim[:, part], near, along, right[:, part], forces, places))
    pairs = {}
    results = [[] for _ in range(NEAR)]
    for step in range(len(opened) + 1):
        if step < len(opened):
            _, _, near, along, right, _, _ = opened[step]
            pairs[step] = dot(near, right), dot(along, right)
        if step:
            slot, aim, _, _, _, forces, places = opened[step - 1]
            both = weights(*pairs.pop(step - 1))
            direct = dot(forces, jnp.concatenate(both[:2], axis=0))
            moment = dot(places, jnp.concatenate(both[2:], axis=0))
            results[slot].append(finish(aim, direct, moment))
    results = [
        jnp.where(slot < count_ref[0], jnp.concatenate(results[slot], axis=1), 0.0)
        for slot in range(NEAR)
    ]
    rows = lax.broadcasted_iota(jnp.int32, (cells, 1), 0)
    return [
        sum(
            jnp.where(rows == target_ref[0, slot], results[slot][k : k + 1], 0.0)
            for slot in range(NEAR)
        )
        for k in range(3)
    ]


def near_kernel(target_ref, owner_ref, cell_ref, count_ref, points_ref, *refs, spread, move):
    pool_refs, (rest_ref, stiffness_ref, out_ref, rows_ref, move_ref) = refs[:-5], refs[-5:]
    gather(owner_ref, cell_ref, pool_refs, rows_ref, spread)
    stiffness = split(stiffness_ref[...])
    near = near_sums(target_ref, count_ref, points_ref, rest_ref, stiffness, rows_ref, move_ref)
    for k in range(3):
        out_ref[k] = points_ref[k] + TIME_STEP * near[k] if move else near[k]


def boxes(main, ends, center, template, radius, per_row):
    count = main[0].shape[0]
    tail_lanes = template[2]
    rows = []
    for k in range(3):
        place_main = center[k] + radius * template[0][k : k + 1]
        place_ends = jnp.where(tail_lanes, center[k] + radius * template[1][k : k + 1], 0.0)
        rows.append((place_main, place_ends))
    for k in range(3):
        rows.append((main[k], ends[k]))
    packed = []
    for whole, part in rows:
        turn = lax.broadcasted_iota(jnp.int32, (count, 1), 0) % per_row[0]
        shifted = jnp.where(turn == 0, part, 0.0)
        for i in range(1, per_row[0]):
            shifted += jnp.where(turn == i, pltpu.roll(part, per_row[1] * i, axis=1), 0.0)
        packed.append(
            [whole]
            + [
                jnp.sum(shifted[a : min(a + per_row[0], count)], axis=0, keepdims=True)
                for a in range(0, count, per_row[0])
            ]
        )
    return packed


def far_checks(
    told_ref, m2m_ref, template_ref, wide_ref, sums_ref, group_ref, source_ref, groups, devs
):
    q = template_ref.shape[1]
    tail = q - LANES
    per_row = (LANES // tail, tail)
    group = lax.axis_index("grp")
    dev = lax.axis_index("dev")
    tail_lanes = lax.broadcasted_iota(jnp.int32, (1, LANES), 1) < tail

    wide_ref[...] = jnp.zeros_like(wide_ref)
    wide_ref[0:3, :q] = template_ref[...]
    template = (wide_ref[:, :LANES], wide_ref[:, LANES:], tail_lanes)

    first = group * devs
    own_rows = [told_ref[pl.ds(first, devs), k, :] for k in range(4)]
    others = lax.broadcasted_iota(jnp.int32, (devs, 1), 0) != dev
    inner = boxes(
        [jnp.where(others, own_rows[k], 0.0) for k in range(3)],
        [jnp.where(others, ends_of(own_rows[3], k, tail), 0.0) for k in range(3)],
        [own_rows[3][:, 3 * tail + k : 3 * tail + k + 1] for k in range(3)],
        template,
        DEVICE_RADIUS,
        per_row,
    )

    span = up8(groups)
    sums_ref[...] = jnp.zeros_like(sums_ref)
    for h in range(groups):
        sums_ref[h] = jnp.sum(told_ref[h * devs : (h + 1) * devs, 0:4, :], axis=0)
    sum_rows = [sums_ref[:, k, :] for k in range(4)]
    for k in range(3):
        group_ref[span * k : span * (k + 1), :LANES] = sum_rows[k]
        group_ref[span * k : span * (k + 1), LANES:] = ends_of(sum_rows[3], k, tail)
    shifted = dot3(group_ref[:, :q], split(m2m_ref[...]))
    group_ref[:, :q] = shifted
    other_groups = lax.broadcasted_iota(jnp.int32, (span, 1), 0) != group
    outer = boxes(
        [
            jnp.where(other_groups, group_ref[span * k : span * (k + 1), :LANES], 0.0)
            for k in range(3)
        ],
        [
            jnp.where(other_groups, group_ref[span * k : span * (k + 1), LANES:], 0.0)
            for k in range(3)
        ],
        [sum_rows[3][:, 3 * tail + k : 3 * tail + k + 1] / devs for k in range(3)],
        template,
        GROUP_RADIUS,
        per_row,
    )
    source_ref[...] = jnp.zeros_like(source_ref)
    rows = 0
    center_row = told_ref[pl.ds(first + dev, 1), 3, :]
    centers = [center_row[:, 3 * tail + k : 3 * tail + k + 1] for k in range(3)]
    for part, count in ((inner, devs), (outer, groups)):
        ends = -(-count // per_row[0])
        for index in range(6):
            shift = centers[index] if index < 3 else 0.0
            source_ref[rows : rows + count, index, :] = part[index][0][:count] - shift
            for j in range(ends):
                at = rows + count + j
                source_ref[at : at + 1, index, :] = part[index][1 + j] - shift
        rows += count + ends
    tall = up8(up8(q) // 2) * 2
    targets = CHECK_RADIUS * wide_ref[0:3, :]
    left = jnp.transpose(stack_left(target_rows(targets)))[:tall].astype(jnp.bfloat16)
    targets = targets[:, :tall]
    contract = functools.partial(
        lax.dot_general,
        dimension_numbers=NT,
        preferred_element_type=jnp.float32,
    )
    dot = functools.partial(jnp.dot, preferred_element_type=jnp.float32)
    direct = jnp.zeros((2 * SUB, tall), jnp.float32)
    moment = jnp.zeros((2 * SUB, tall), jnp.float32)
    count = source_ref.shape[0] // BATCH
    opened, weighed = {}, {}
    for step in range(count + LAG + LEAD):
        if step < count:
            block = jnp.concatenate(
                [source_ref[step * BATCH + i] for i in range(BATCH)], axis=1
            )
            place, force = block[0:3], block[3:6]
            opened[step] = place, force, *(
                dot(left, stack_right(rows).astype(jnp.bfloat16))
                for rows in source_rows(place, force)
            )
        if 0 <= step - LEAD < count:
            place, force, *pair = opened.pop(step - LEAD)
            weighed[step - LEAD] = place, force, weights(*pair)
        if 0 <= step - LEAD - LAG < count:
            place, force, both = weighed.pop(step - LEAD - LAG)
            forces = stack_pair(rows8([force]))
            places = stack_pair(rows8([place, jnp.ones_like(place[:1])]))
            direct += contract(twice(forces), jnp.concatenate(both[:2], axis=1))
            moment += contract(twice(places), jnp.concatenate(both[2:], axis=1))
    return finish(targets, direct, moment)[:, :q]


def surface_of(checks, down_ref):
    return dot3(rows8([checks]), split(down_ref[...]))


def turn_kernel(
    told_ref,
    partial_ref,
    m2m_ref,
    template_ref,
    down_ref,
    rest_ref,
    up_ref,
    stiffness_ref,
    points_ref,
    out_ref,
    *refs,
    groups,
    devs,
):
    rows_ref, flat_ref = refs[-2:]
    checks = far_checks(told_ref, m2m_ref, template_ref, *refs[:-2], groups, devs)
    surface = surface_of(checks, down_ref)
    points = [partial_ref[k] + TIME_STEP * surface[k : k + 1] for k in range(3)]
    for k in range(3):
        points_ref[k] = points[k]
    centers = membrane_rows(points, rest_ref, rows_ref)
    linear = dot3(rows_ref[...], split(stiffness_ref[...]))
    equivalent_rows(linear, up_ref[...], flat_ref)
    message = pack(flat_ref, up_ref.shape[0], centers)
    out_ref[...] = jnp.broadcast_to(message[None], out_ref.shape)


def last_kernel(
    told_ref,
    points_ref,
    near_ref,
    m2m_ref,
    template_ref,
    down_ref,
    points_out_ref,
    velocity_ref,
    *refs,
    groups,
    devs,
):
    checks = far_checks(told_ref, m2m_ref, template_ref, *refs, groups, devs)
    surface = surface_of(checks, down_ref)
    for k in range(3):
        velocity = surface[k : k + 1] + near_ref[k]
        velocity_ref[k] = velocity
        points_out_ref[k] = points_ref[k] + TIME_STEP * velocity


VMEM = pl.BlockSpec(memory_space=pltpu.VMEM)
SMEM = pl.BlockSpec(memory_space=pltpu.SMEM)


def float32(*shape):
    return jax.ShapeDtypeStruct(shape, jnp.float32)


def scratch(*shape):
    return pltpu.VMEM(shape, jnp.float32)


def call(kernel, in_specs, outs, scratch_shapes, gflop, mib=24):
    return pl.pallas_call(
        kernel,
        in_specs=in_specs,
        out_shape=tuple(outs),
        out_specs=(VMEM,) * len(outs),
        scratch_shapes=scratch_shapes,
        compiler_params=pltpu.CompilerParams(vmem_limit_bytes=mib * 2**20),
        cost_estimate=pl.CostEstimate(
            flops=gflop * 10**9, bytes_accessed=10**6, transcendentals=0
        ),
    )


def body(
    positions,
    rest_shape,
    stiffness,
    up_map,
    down_map,
    m2m,
    box_template,
    near_target,
    near_owner,
    near_cell,
    near_count,
):
    devs = lax.axis_size("dev")
    groups = lax.axis_size("grp")
    everyone = groups * devs
    cells, size = positions.shape[1:]
    q = up_map.shape[1]
    spread = devs == 8
    pools = 8 if spread else 1
    span = up8(groups)
    tail_boxes = LANES // (q - LANES)
    source_count = devs + groups + -(-devs // tail_boxes) + -(-groups // tail_boxes)
    cell_array = float32(3, cells, size)
    up_rows = up_map.T
    lists = (near_target, near_owner, near_cell, near_count)
    far_scratch = [
        scratch(SUB, 2 * LANES),
        scratch(span, 4, LANES),
        scratch(3 * span, 2 * LANES),
        scratch(-(-source_count // BATCH) * BATCH, SUB, LANES),
    ]
    near_scratch = [scratch(NEAR * SUB, size), scratch(NEAR * SUB, size)]
    membrane_scratch = [scratch(3 * SUB, size), scratch(SUB, 2 * LANES)]

    first = call(first_kernel, [VMEM] * 5, [float32(everyone, 4, LANES)], membrane_scratch, 1)
    blank = call(blank_kernel, [], [float32(SUB, LANES)], [], 40)

    def near(points, pool, move):
        kernel = functools.partial(near_kernel, spread=spread, move=move)
        specs = [SMEM] * 4 + [VMEM] * (1 + pools + 2)
        run = call(kernel, specs, [cell_array], near_scratch, 4)
        return run(*lists, points, *pool, rest_shape, stiffness)[0]

    turn = call(
        functools.partial(turn_kernel, groups=groups, devs=devs),
        [VMEM] * 8,
        [cell_array, float32(everyone, 4, LANES)],
        far_scratch + membrane_scratch,
        3,
    )
    last = call(
        functools.partial(last_kernel, groups=groups, devs=devs),
        [VMEM] * 6,
        [cell_array, cell_array],
        far_scratch,
        3,
    )

    def to(array, mask):
        return lax.ppermute(array, "dev", [(j, j ^ mask) for j in range(devs)])

    def pool_of(array):
        if not spread:
            copies = jnp.broadcast_to(array[None], (devs,) + array.shape)
            return [lax.all_to_all(copies, "dev", 0, 0)]
        reached = {0: array}
        for mask in (6, 4, 2):
            reached[mask] = to(array, mask)
        reached[1] = to(array, 1)
        for mask in (2, 4, 6):
            reached[mask + 1] = to(reached[mask], 1)
        return [reached[mask] for mask in range(8)]

    def tell(message):
        return lax.all_to_all(message, ("grp", "dev"), 0, 0)

    (empty,) = blank()
    pool = pool_of(positions)
    (message,) = first(empty, positions, rest_shape, up_rows, stiffness)
    told = tell(message)
    partial = near(positions, pool, True)
    points, message = turn(
        told, partial, m2m, box_template, down_map, rest_shape, up_rows, stiffness
    )
    pool = pool_of(points)
    told = tell(message)
    close = near(points, pool, False)
    return last(told, points, close, m2m, box_template, down_map)


def solution(mesh):
    both = ("grp", "dev")
    return jax.shard_map(
        body,
        mesh=mesh,
        in_specs=(P(None, both, None),) + (P(),) * 6 + (P(both, None),) * 3 + (P(both),),
        out_specs=(P(None, both, None), P(None, both, None)),
        check_vma=False,
    )
```

```python
import functools

import jax
import jax.numpy as jnp
from jax import lax
from jax.experimental import pallas as pl
from jax.experimental.pallas import tpu as pltpu
from jax.sharding import PartitionSpec as P


NEAR = 2

EPSILON_SQ = 0.25
VISCOSITY = 0.039788735772973836
TIME_STEP = 0.1
SKALAK_HARDEN = 2.0
CHECK_RADIUS = 1.0
DEVICE_RADIUS = 1.5
GROUP_RADIUS = 6.0

LANES = 128
SUB = 8
BATCH = 2
WIDTH = 128
LAG = 1
LEAD = 1


def up8(n):
    return -(-n // SUB) * SUB


def split(a):
    high = a.astype(jnp.bfloat16)
    low = (a - high.astype(jnp.float32)).astype(jnp.bfloat16)
    return high, low


NN = (((1,), (0,)), ((), ()))
NT = (((1,), (1,)), ((), ()))


def dot3(a, b_parts, dims=NN):
    dot = functools.partial(
        lax.dot_general, dimension_numbers=dims, preferred_element_type=jnp.float32
    )
    rows = a.shape[0]
    first = a.astype(jnp.bfloat16).astype(jnp.float32)
    both = jnp.concatenate([first, a - first], axis=0).astype(jnp.bfloat16)
    high = dot(both, b_parts[0])
    return high[:rows] + (high[rows:] + dot(first.astype(jnp.bfloat16), b_parts[1]))


def harden(linear, stretch):
    return -linear * (1.0 + SKALAK_HARDEN * stretch / (1.0 + stretch))


def parts3(a):
    first = a.astype(jnp.bfloat16).astype(jnp.float32)
    rest = a - first
    second = rest.astype(jnp.bfloat16).astype(jnp.float32)
    return first, second, rest - second


def stack_left(a):
    first, second, third = parts3(a)
    return jnp.concatenate([first, first, first, second, second, third], axis=0)


def stack_right(a):
    first, second, third = parts3(a)
    return jnp.concatenate([first, second, third, first, second, first], axis=0)


def stack_pair(a):
    first, second, _ = parts3(a)
    return jnp.concatenate([first, second], axis=0).astype(jnp.bfloat16)


def rows8(rows):
    size = rows[0].shape[1]
    count = sum(row.shape[0] for row in rows)
    return jnp.concatenate(rows + [jnp.zeros((SUB - count, size), jnp.float32)], axis=0)


def square_of(place):
    return jnp.sum(place * place, axis=0, keepdims=True)


def target_rows(place):
    return rows8([place, square_of(place), jnp.ones_like(place[:1])])


def source_rows(place, force):
    near = rows8(
        [-2.0 * place, jnp.ones_like(place[:1]), square_of(place) + EPSILON_SQ]
    )
    along = rows8(
        [
            force,
            jnp.zeros_like(place[:1]),
            -jnp.sum(place * force, axis=0, keepdims=True),
        ]
    )
    return near, along


def weights(shifted, along):
    root = lax.rsqrt(jnp.maximum(shifted, EPSILON_SQ))
    inverse = root * root * root
    return split(root + EPSILON_SQ * inverse) + split(along * inverse)


def twice(a):
    return jnp.concatenate([a, a], axis=1)


def finish(place, direct, moment):
    direct = direct[:SUB] + direct[SUB:]
    moment = moment[:SUB] + moment[SUB:]
    return VISCOSITY * (direct[0:3] + place * moment[3:4] - moment[0:3])


def membrane_rows(points, rest_ref, rows_ref):
    cells = points[0].shape[0]
    rows_ref[...] = jnp.zeros_like(rows_ref)
    centers = []
    for k in range(3):
        mean = jnp.mean(points[k], axis=1, keepdims=True)
        rows_ref[SUB * k : SUB * k + cells, :] = points[k] - mean - rest_ref[k : k + 1, :]
        centers.append(jnp.mean(mean, axis=0, keepdims=True))
    return centers


def equivalent_rows(linear, up, flat_ref):
    parts = [linear[SUB * k : SUB * (k + 1)] for k in range(3)]
    stretch = parts[0] * parts[0] + parts[1] * parts[1] + parts[2] * parts[2]
    sums = [jnp.sum(harden(part, stretch), axis=0, keepdims=True) for part in parts]
    flat_ref[...] = jnp.zeros_like(flat_ref)
    flat_ref[:, : up.shape[0]] = dot3(rows8(sums), split(up), NT)


def pack(flat_ref, q, centers=()):
    tail = q - LANES
    ends = flat_ref[:, LANES:]
    last = ends[0:1]
    lane = lax.broadcasted_iota(jnp.int32, (1, LANES), 1)
    for k in range(1, 3):
        last = last + pltpu.roll(ends[k : k + 1], tail * k, axis=1)
    for k, center in enumerate(centers):
        last = jnp.where(lane == 3 * tail + k, center, last)
    return jnp.concatenate([flat_ref[0:3, :LANES], last], axis=0)


def ends_of(row, k, tail):
    lane = lax.broadcasted_iota(jnp.int32, (1, LANES), 1)
    moved = pltpu.roll(row, LANES - tail * k, axis=1) if k else row
    return jnp.where(lane < tail, moved, 0.0)


def blank_kernel(out_ref):
    out_ref[...] = jnp.zeros_like(out_ref)


def first_kernel(
    blank_ref, points_ref, rest_ref, up_ref, stiffness_ref, out_ref, rows_ref, flat_ref
):
    centers = membrane_rows([points_ref[k] for k in range(3)], rest_ref, rows_ref)
    linear = dot3(rows_ref[...], split(stiffness_ref[...]))
    equivalent_rows(linear, up_ref[...], flat_ref)
    message = pack(flat_ref, up_ref.shape[0], centers) + blank_ref[0:4, :]
    out_ref[...] = jnp.broadcast_to(message[None], out_ref.shape)


def pick(block, row):
    rows = lax.broadcasted_iota(jnp.int32, (block.shape[0], 1), 0)
    return jnp.sum(jnp.where(rows == row, block, 0.0), axis=0, keepdims=True)


def gather(owner_ref, cell_ref, pool_refs, rows_ref, spread):
    me = lax.axis_index("dev")
    rows_ref[...] = jnp.zeros_like(rows_ref)
    for slot in range(NEAR):
        cell = cell_ref[0, slot]
        owner = owner_ref[0, slot]
        if spread:
            place = owner ^ me
            for k in range(3):
                chosen = pool_refs[0][k]
                for mask in range(1, len(pool_refs)):
                    chosen = jnp.where(place == mask, pool_refs[mask][k], chosen)
                rows_ref[SUB * slot + k : SUB * slot + k + 1, :] = pick(chosen, cell)
        else:
            for k in range(3):
                rows_ref[SUB * slot + k : SUB * slot + k + 1, :] = pick(
                    pool_refs[0][owner, k], cell
                )


def near_sums(target_ref, count_ref, points_ref, rest_ref, stiffness, rows_ref, move_ref):
    cells, size = points_ref.shape[1:]
    sources = rows_ref[...]
    move_ref[...] = jnp.zeros_like(move_ref)
    for slot in range(NEAR):
        own = sources[SUB * slot : SUB * slot + 3]
        mean = jnp.mean(own, axis=1, keepdims=True)
        move_ref[SUB * slot : SUB * slot + 3, :] = own - mean - rest_ref[...]
    linear = dot3(move_ref[...], stiffness)
    square = linear * linear
    dot = functools.partial(jnp.dot, preferred_element_type=jnp.float32)
    opened = []
    for slot in range(NEAR):
        part = linear[SUB * slot : SUB * slot + 3]
        stretch = jnp.sum(square[SUB * slot : SUB * slot + 3], axis=0, keepdims=True)
        force = harden(part, stretch)
        aim = jnp.concatenate([pick(points_ref[k], target_ref[0, slot]) for k in range(3)], axis=0)
        center = jnp.mean(aim, axis=1, keepdims=True)
        aim = aim - center
        place = sources[SUB * slot : SUB * slot + 3] - center
        near, along = (
            jnp.transpose(stack_left(rows)).astype(jnp.bfloat16)
            for rows in source_rows(place, force)
        )
        right = stack_right(target_rows(aim)).astype(jnp.bfloat16)
        forces = twice(stack_pair(rows8([force])))
        places = twice(stack_pair(rows8([place, jnp.ones_like(place[:1])])))
        for lane in range(0, size, WIDTH):
            part = slice(lane, min(lane + WIDTH, size))
            opened.append((slot, aim[:, part], near, along, right[:, part], forces, places))
    pairs = {}
    results = [[] for _ in range(NEAR)]
    for step in range(len(opened) + 1):
        if step < len(opened):
            _, _, near, along, right, _, _ = opened[step]
            pairs[step] = dot(near, right), dot(along, right)
        if step:
            slot, aim, _, _, _, forces, places = opened[step - 1]
            both = weights(*pairs.pop(step - 1))
            direct = dot(forces, jnp.concatenate(both[:2], axis=0))
            moment = dot(places, jnp.concatenate(both[2:], axis=0))
            results[slot].append(finish(aim, direct, moment))
    results = [
        jnp.where(slot < count_ref[0], jnp.concatenate(results[slot], axis=1), 0.0)
        for slot in range(NEAR)
    ]
    rows = lax.broadcasted_iota(jnp.int32, (cells, 1), 0)
    return [
        sum(
            jnp.where(rows == target_ref[0, slot], results[slot][k : k + 1], 0.0)
            for slot in range(NEAR)
        )
        for k in range(3)
    ]


def near_kernel(target_ref, owner_ref, cell_ref, count_ref, points_ref, *refs, spread, move):
    pool_refs, (rest_ref, stiffness_ref, out_ref, rows_ref, move_ref) = refs[:-5], refs[-5:]
    gather(owner_ref, cell_ref, pool_refs, rows_ref, spread)
    stiffness = split(stiffness_ref[...])
    near = near_sums(target_ref, count_ref, points_ref, rest_ref, stiffness, rows_ref, move_ref)
    for k in range(3):
        out_ref[k] = points_ref[k] + TIME_STEP * near[k] if move else near[k]


def boxes(main, ends, center, template, radius, per_row):
    count = main[0].shape[0]
    tail_lanes = template[2]
    rows = []
    for k in range(3):
        place_main = center[k] + radius * template[0][k : k + 1]
        place_ends = jnp.where(tail_lanes, center[k] + radius * template[1][k : k + 1], 0.0)
        rows.append((place_main, place_ends))
    for k in range(3):
        rows.append((main[k], ends[k]))
    packed = []
    for whole, part in rows:
        turn = lax.broadcasted_iota(jnp.int32, (count, 1), 0) % per_row[0]
        shifted = jnp.where(turn == 0, part, 0.0)
        for i in range(1, per_row[0]):
            shifted += jnp.where(turn == i, pltpu.roll(part, per_row[1] * i, axis=1), 0.0)
        packed.append(
            [whole]
            + [
                jnp.sum(shifted[a : min(a + per_row[0], count)], axis=0, keepdims=True)
                for a in range(0, count, per_row[0])
            ]
        )
    return packed


def far_checks(
    told_ref, m2m_ref, template_ref, wide_ref, sums_ref, group_ref, source_ref, groups, devs
):
    q = template_ref.shape[1]
    tail = q - LANES
    per_row = (LANES // tail, tail)
    group = lax.axis_index("grp")
    dev = lax.axis_index("dev")
    tail_lanes = lax.broadcasted_iota(jnp.int32, (1, LANES), 1) < tail

    wide_ref[...] = jnp.zeros_like(wide_ref)
    wide_ref[0:3, :q] = template_ref[...]
    template = (wide_ref[:, :LANES], wide_ref[:, LANES:], tail_lanes)

    first = group * devs
    own_rows = [told_ref[pl.ds(first, devs), k, :] for k in range(4)]
    others = lax.broadcasted_iota(jnp.int32, (devs, 1), 0) != dev
    inner = boxes(
        [jnp.where(others, own_rows[k], 0.0) for k in range(3)],
        [jnp.where(others, ends_of(own_rows[3], k, tail), 0.0) for k in range(3)],
        [own_rows[3][:, 3 * tail + k : 3 * tail + k + 1] for k in range(3)],
        template,
        DEVICE_RADIUS,
        per_row,
    )

    span = up8(groups)
    sums_ref[...] = jnp.zeros_like(sums_ref)
    for h in range(groups):
        sums_ref[h] = jnp.sum(told_ref[h * devs : (h + 1) * devs, 0:4, :], axis=0)
    sum_rows = [sums_ref[:, k, :] for k in range(4)]
    for k in range(3):
        group_ref[span * k : span * (k + 1), :LANES] = sum_rows[k]
        group_ref[span * k : span * (k + 1), LANES:] = ends_of(sum_rows[3], k, tail)
    shifted = dot3(group_ref[:, :q], split(m2m_ref[...]))
    group_ref[:, :q] = shifted
    other_groups = lax.broadcasted_iota(jnp.int32, (span, 1), 0) != group
    outer = boxes(
        [
            jnp.where(other_groups, group_ref[span * k : span * (k + 1), :LANES], 0.0)
            for k in range(3)
        ],
        [
            jnp.where(other_groups, group_ref[span * k : span * (k + 1), LANES:], 0.0)
            for k in range(3)
        ],
        [sum_rows[3][:, 3 * tail + k : 3 * tail + k + 1] / devs for k in range(3)],
        template,
        GROUP_RADIUS,
        per_row,
    )
    source_ref[...] = jnp.zeros_like(source_ref)
    rows = 0
    center_row = told_ref[pl.ds(first + dev, 1), 3, :]
    centers = [center_row[:, 3 * tail + k : 3 * tail + k + 1] for k in range(3)]
    for part, count in ((inner, devs), (outer, groups)):
        ends = -(-count // per_row[0])
        for index in range(6):
            shift = centers[index] if index < 3 else 0.0
            source_ref[rows : rows + count, index, :] = part[index][0][:count] - shift
            for j in range(ends):
                at = rows + count + j
                source_ref[at : at + 1, index, :] = part[index][1 + j] - shift
        rows += count + ends
    tall = up8(up8(q) // 2) * 2
    targets = CHECK_RADIUS * wide_ref[0:3, :]
    left = jnp.transpose(stack_left(target_rows(targets)))[:tall].astype(jnp.bfloat16)
    targets = targets[:, :tall]
    contract = functools.partial(
        lax.dot_general,
        dimension_numbers=NT,
        preferred_element_type=jnp.float32,
    )
    dot = functools.partial(jnp.dot, preferred_element_type=jnp.float32)
    direct = jnp.zeros((2 * SUB, tall), jnp.float32)
    moment = jnp.zeros((2 * SUB, tall), jnp.float32)
    count = source_ref.shape[0] // BATCH
    opened, weighed = {}, {}
    for step in range(count + LAG + LEAD):
        if step < count:
            block = jnp.concatenate(
                [source_ref[step * BATCH + i] for i in range(BATCH)], axis=1
            )
            place, force = block[0:3], block[3:6]
            opened[step] = place, force, *(
                dot(left, stack_right(rows).astype(jnp.bfloat16))
                for rows in source_rows(place, force)
            )
        if 0 <= step - LEAD < count:
            place, force, *pair = opened.pop(step - LEAD)
            weighed[step - LEAD] = place, force, weights(*pair)
        if 0 <= step - LEAD - LAG < count:
            place, force, both = weighed.pop(step - LEAD - LAG)
            forces = stack_pair(rows8([force]))
            places = stack_pair(rows8([place, jnp.ones_like(place[:1])]))
            direct += contract(twice(forces), jnp.concatenate(both[:2], axis=1))
            moment += contract(twice(places), jnp.concatenate(both[2:], axis=1))
    return finish(targets, direct, moment)[:, :q]


def surface_of(checks, down_ref):
    return dot3(rows8([checks]), split(down_ref[...]))


def turn_kernel(
    told_ref,
    partial_ref,
    m2m_ref,
    template_ref,
    down_ref,
    rest_ref,
    up_ref,
    stiffness_ref,
    points_ref,
    out_ref,
    *refs,
    groups,
    devs,
):
    rows_ref, flat_ref = refs[-2:]
    checks = far_checks(told_ref, m2m_ref, template_ref, *refs[:-2], groups, devs)
    surface = surface_of(checks, down_ref)
    points = [partial_ref[k] + TIME_STEP * surface[k : k + 1] for k in range(3)]
    for k in range(3):
        points_ref[k] = points[k]
    centers = membrane_rows(points, rest_ref, rows_ref)
    linear = dot3(rows_ref[...], split(stiffness_ref[...]))
    equivalent_rows(linear, up_ref[...], flat_ref)
    message = pack(flat_ref, up_ref.shape[0], centers)
    out_ref[...] = jnp.broadcast_to(message[None], out_ref.shape)


def last_kernel(
    told_ref,
    points_ref,
    near_ref,
    m2m_ref,
    template_ref,
    down_ref,
    points_out_ref,
    velocity_ref,
    *refs,
    groups,
    devs,
):
    checks = far_checks(told_ref, m2m_ref, template_ref, *refs, groups, devs)
    surface = surface_of(checks, down_ref)
    for k in range(3):
        velocity = surface[k : k + 1] + near_ref[k]
        velocity_ref[k] = velocity
        points_out_ref[k] = points_ref[k] + TIME_STEP * velocity


VMEM = pl.BlockSpec(memory_space=pltpu.VMEM)
SMEM = pl.BlockSpec(memory_space=pltpu.SMEM)


def float32(*shape):
    return jax.ShapeDtypeStruct(shape, jnp.float32)


def scratch(*shape):
    return pltpu.VMEM(shape, jnp.float32)


def call(kernel, in_specs, outs, scratch_shapes, gflop, mib=24):
    return pl.pallas_call(
        kernel,
        in_specs=in_specs,
        out_shape=tuple(outs),
        out_specs=(VMEM,) * len(outs),
        scratch_shapes=scratch_shapes,
        compiler_params=pltpu.CompilerParams(vmem_limit_bytes=mib * 2**20),
        cost_estimate=pl.CostEstimate(
            flops=gflop * 10**9, bytes_accessed=10**6, transcendentals=0
        ),
    )


def body(
    positions,
    rest_shape,
    stiffness,
    up_map,
    down_map,
    m2m,
    box_template,
    near_target,
    near_owner,
    near_cell,
    near_count,
):
    devs = lax.axis_size("dev")
    groups = lax.axis_size("grp")
    everyone = groups * devs
    cells, size = positions.shape[1:]
    q = up_map.shape[1]
    spread = devs == 8
    pools = 8 if spread else 1
    span = up8(groups)
    tail_boxes = LANES // (q - LANES)
    source_count = devs + groups + -(-devs // tail_boxes) + -(-groups // tail_boxes)
    cell_array = float32(3, cells, size)
    up_rows = up_map.T
    lists = (near_target, near_owner, near_cell, near_count)
    far_scratch = [
        scratch(SUB, 2 * LANES),
        scratch(span, 4, LANES),
        scratch(3 * span, 2 * LANES),
        scratch(-(-source_count // BATCH) * BATCH, SUB, LANES),
    ]
    near_scratch = [scratch(NEAR * SUB, size), scratch(NEAR * SUB, size)]
    membrane_scratch = [scratch(3 * SUB, size), scratch(SUB, 2 * LANES)]

    first = call(first_kernel, [VMEM] * 5, [float32(everyone, 4, LANES)], membrane_scratch, 1)
    blank = call(blank_kernel, [], [float32(SUB, LANES)], [], 40)

    def near(points, pool, move):
        kernel = functools.partial(near_kernel, spread=spread, move=move)
        specs = [SMEM] * 4 + [VMEM] * (1 + pools + 2)
        run = call(kernel, specs, [cell_array], near_scratch, 4)
        return run(*lists, points, *pool, rest_shape, stiffness)[0]

    turn = call(
        functools.partial(turn_kernel, groups=groups, devs=devs),
        [VMEM] * 8,
        [cell_array, float32(everyone, 4, LANES)],
        far_scratch + membrane_scratch,
        3,
    )
    last = call(
        functools.partial(last_kernel, groups=groups, devs=devs),
        [VMEM] * 6,
        [cell_array, cell_array],
        far_scratch,
        3,
    )

    def to(array, mask):
        return lax.ppermute(array, "dev", [(j, j ^ mask) for j in range(devs)])

    def pool_of(array):
        if not spread:
            copies = jnp.broadcast_to(array[None], (devs,) + array.shape)
            return [lax.all_to_all(copies, "dev", 0, 0)]
        reached = {0: array}
        for mask in (6, 4, 2):
            reached[mask] = to(array, mask)
        reached[1] = to(array, 1)
        for mask in (2, 4, 6):
            reached[mask + 1] = to(reached[mask], 1)
        return [reached[mask] for mask in range(8)]

    def tell(message):
        return lax.all_to_all(message, ("grp", "dev"), 0, 0)

    (empty,) = blank()
    pool = pool_of(positions)
    (message,) = first(empty, positions, rest_shape, up_rows, stiffness)
    told = tell(message)
    partial = near(positions, pool, True)
    points, message = turn(
        told, partial, m2m, box_template, down_map, rest_shape, up_rows, stiffness
    )
    pool = pool_of(points)
    told = tell(message)
    close = near(points, pool, False)
    return last(told, points, close, m2m, box_template, down_map)


def solution(mesh):
    both = ("grp", "dev")
    return jax.shard_map(
        body,
        mesh=mesh,
        in_specs=(P(None, both, None),) + (P(),) * 6 + (P(both, None),) * 3 + (P(both),),
        out_specs=(P(None, both, None), P(None, both, None)),
        check_vma=False,
    )
```
